32 devices in a mesh: groups: 2 (over y), patch: 8 (over z, x), batch: 2 (over core).
Axes of the slice: x: 2, y: 2, z: 4, core: 2. Of those that a mesh axis runs over, the one named last changes fastest.
Arguments:
- subjects: bfloat16 [2048, 3, 20480], P(('groups', 'batch'), None, 'patch'), parts along dimension 0, may hold values from -6 to 6
- basis_modes: bfloat16 [3, 40960, 128], P(None, ('groups', 'patch')), parts along dimension 1, may hold values from -21 to 21
- laplace_blocks: bfloat16 [320, 4, 64, 64], P('patch'), may hold values from -0.29882812 to 0.29882812
- columns: int32 [320, 4], P('patch'), may hold values from 0 to 319, as said below
Outputs:
- scores: float32 [2048, 128], P(('groups', 'batch')), parts along dimension 0
- new_modes: bfloat16 [3, 40960, 128], P(None, ('groups', 'patch')), parts along dimension 1
- mode_norms: float32 [256], P('groups'), parts along dimension 0
The draws below stay inside these ranges and needn't reach their ends.
There are 2 independent parts, one for each index of `groups`. The reference program is written for one: setup_inputs(seed, part) draws one part's arguments, and reference() takes and returns one part's arrays. A program takes and returns all parts, laid end to end along the dimension named above; an argument that names none is the same for every part. Nothing has to cross between parts.
Inputs may be any that keep to these rules, and one draw needn't show every extreme that they name: columns[i, 0] = i; with 40 blocks a patch, an entry of block row i lies in i's own patch, except that in the last 4 block rows of a patch an entry may also lie among the first 4 blocks of the next patch; entries of a row may repeat.
All inputs are finite; a program needn't handle non-finite values.
Results may differ from the reference program's by a relative error of at most 0.0034.
Values may be sent and summed in bfloat16 or wider, within the bound.
A program may use at most 192 MiB of HBM per device.

```python
import math
import jax
import jax.numpy as jnp
from jax import lax

K = 128
VERT_DEV = 2560
NB = 4
GHOST = 4
BLK_DEV = 40
VERTS = 20480
BLOCKS = 320
COORDS = 61440
BATCH = 1024
N_PATCH = 8


def draw_columns(key, part):
    rows_id = jnp.arange(BLOCKS, dtype=jnp.int32)
    patch_of = rows_id // BLK_DEV
    local_row = rows_id % BLK_DEV
    last_patch = BLOCKS // BLK_DEV - 1
    raw_cols = jax.random.randint(key, (BLOCKS, NB), 0, 2 * BLK_DEV * GHOST, dtype=jnp.int32)
    interior = patch_of[:, None] * BLK_DEV + raw_cols % BLK_DEV
    folded = raw_cols % (2 * GHOST)
    edge_own = patch_of[:, None] * BLK_DEV + BLK_DEV - GHOST + folded % GHOST
    edge_next = (patch_of[:, None] + 1) * BLK_DEV + folded - GHOST
    reach_next = (folded >= GHOST) & (patch_of[:, None] != last_patch)
    edge_pick = jnp.where(reach_next, edge_next, edge_own)
    is_edge = (local_row >= BLK_DEV - GHOST)[:, None]
    picked = jnp.where(is_edge, edge_pick, interior)
    slot_id = jnp.arange(NB, dtype=jnp.int32)[None, :]
    return jnp.where(slot_id == 0, rows_id[:, None], picked).astype(jnp.int32)


def draw_basis_modes(key, part):
    key_base, key_rough, key_col = jax.random.split(key, 3)
    position = jnp.arange(VERTS, dtype=jnp.float32) / VERTS
    ramp = jnp.sqrt((1.0 + 9.0 * position) / 5.5)
    rough = jnp.exp(jax.random.uniform(key_rough, (3, VERTS, 1), jnp.float32, -0.4, 0.4))
    base = jnp.clip(jax.random.normal(key_base, (3, VERTS, K), jnp.float32), -4.0, 4.0)
    col_scale = jnp.exp(jax.random.uniform(key_col, (K,), jnp.float32, math.log(0.25), math.log(2.5)))
    return (base * ramp[None, :, None] * rough * col_scale[None, None, :]).astype(jnp.bfloat16)


def steps_of(rng, extent, shards, least, largest):
    loudness, own = 1.0, jax.random.fold_in(rng, 6)
    for dim, shards_of in shards:
        heights = jnp.exp(jax.random.uniform(jax.random.fold_in(own, dim), (shards_of,), jnp.float32, least / len(shards), largest / len(shards)))
        loudness = loudness * jnp.repeat(heights, extent[dim] // shards_of).reshape([-1 if axis == dim else 1 for axis in range(len(extent))])
    return loudness


def gaussian(own_key, extent, scale, reach, pieces=(), kind=jnp.bfloat16):
    gain = steps_of(own_key, extent, pieces, -0.22, 0.18) if pieces else 1.0
    result = jax.random.normal(own_key, extent, jnp.float32) * scale * gain
    return jnp.minimum(jnp.maximum(result, -reach), reach).astype(kind)


def setup_inputs(seed: int = 0, part: int = 0) -> dict:
    seeds = jax.random.split(jax.random.key(seed), 5)
    part_splits = jax.random.split(jax.random.fold_in(seeds[4], part), 5)
    subjects = gaussian(part_splits[0], (BATCH, 3, VERTS), 1.0, 6.0, ((0, 2), (2, 8)))
    basis_modes = draw_basis_modes(jax.random.fold_in(jax.random.fold_in(seeds[4], part), 71), part)
    laplace_blocks = gaussian(seeds[2], (BLOCKS, NB, 64, 64), 0.05, 0.29882812, ((0, 8),))
    columns = draw_columns(jax.random.fold_in(seeds[4], 71), part)
    return {"subjects": subjects, "basis_modes": basis_modes, "laplace_blocks": laplace_blocks, "columns": columns}


HIGH = lax.Precision.HIGHEST

def reference(subjects, basis_modes, laplace_blocks, columns):
    scale_inv = 1.0 / math.sqrt(COORDS)
    blocks_f = laplace_blocks.astype(jnp.float32)
    weights = basis_modes.astype(jnp.float32)
    grid = weights.reshape(3, BLOCKS, 64, K)
    flat_cols = columns.reshape(-1)
    degree = blocks_f.sum(axis=(1, 3)) + jax.ops.segment_sum(blocks_f.sum(axis=2).reshape(BLOCKS * NB, 64), flat_cols, num_segments=BLOCKS)
    smooth = degree[None, :, :, None] * grid
    for column in range(NB):
        block_n = blocks_f[:, column]
        picked = jnp.take(grid, columns[:, column], axis=1)
        smooth = smooth - jnp.einsum('bij,cbjk->cbik', block_n, picked, precision=HIGH)
        moved = jnp.einsum('bij,cbik->bcjk', block_n, grid, precision=HIGH)
        smooth = smooth - jax.ops.segment_sum(moved, columns[:, column], num_segments=BLOCKS).transpose(1, 0, 2, 3)
    smooth = smooth.reshape(3, VERTS, K)

    def score_step(patch_id, carry):
        offset = (patch_id * VERT_DEV).astype(jnp.int32)
        piece = lax.dynamic_slice_in_dim(subjects, offset, VERT_DEV, 2).astype(jnp.float32)
        wpiece = lax.dynamic_slice_in_dim(weights, offset, VERT_DEV, 1)
        return carry + jnp.einsum('bcv,cvk->bk', piece, wpiece, precision=HIGH)
    scores = lax.fori_loop(0, N_PATCH, score_step, jnp.zeros((BATCH, K), jnp.float32)) * scale_inv
    low = lax.optimization_barrier(scores.astype(jnp.bfloat16)).astype(jnp.float32)

    def update_piece(patch_id):
        offset = (patch_id * VERT_DEV).astype(jnp.int32)
        piece = lax.dynamic_slice_in_dim(subjects, offset, VERT_DEV, 2).astype(jnp.float32)
        wpiece = lax.dynamic_slice_in_dim(weights, offset, VERT_DEV, 1)
        spiece = lax.dynamic_slice_in_dim(smooth, offset, VERT_DEV, 1)
        recon = jnp.einsum('bk,cvk->bcv', low, wpiece, precision=HIGH) * scale_inv
        resid = lax.optimization_barrier((piece - recon).astype(jnp.bfloat16)).astype(jnp.float32)
        hebb = jnp.einsum('bcv,bk->cvk', resid, low, precision=HIGH)
        return wpiece + 4.0 / BATCH * hebb - 0.2 * spiece
    updated = lax.map(update_piece, jnp.arange(N_PATCH, dtype=jnp.int32))
    updated = updated.transpose(1, 0, 2, 3).reshape(3, VERTS, K)
    norms = jnp.sqrt(lax.optimization_barrier(jnp.mean(updated * updated, axis=(0, 1))) + 1e-06)
    return (scores, (updated / norms).astype(jnp.bfloat16), norms)
```

```python
import functools
import math

import jax
import jax.numpy as jnp
from jax import lax
from jax.experimental import pallas as pl
from jax.experimental.pallas import tpu as pltpu
from jax.sharding import PartitionSpec as P

GHOST = 4
WIRE = jnp.bfloat16
MESH = pl.DeviceIdType.MESH
VMEM = pl.BlockSpec(memory_space=pltpu.VMEM)
ANY = pl.BlockSpec(memory_space=pl.ANY)
LIMIT = 62 * 1024 * 1024
FAR = (((1,), (1,)), ((), ()))
DOWN = (((0,), (0,)), ((), ()))


def ds(start, size):
    return pl.ds(pl.multiple_of(start, size), size)


def far_first(n):
    return sorted(range(1, n), key=lambda step: -min(step, n - step))


def dot(a, b):
    return jnp.dot(a, b, preferred_element_type=jnp.float32)


def step_kernel(
    scale, rate, coord_count,
    planes, modes, blocks, columns, table,
    updated, norms, low,
    held, wide, tail, lap, cols, links, part, outbox, land, run, acc, base, turned, flipped,
    outgo, income, carry, extra, slots,
    load_m, load_s, load_x, send_a, recv_a, send_b, recv_b, edge_sem, carry_sem,
    send_u, recv_u, send_g, recv_g, send_n, recv_n,
):
    n, me = lax.axis_size("patch"), lax.axis_index("patch")
    pair, half = lax.axis_size("batch"), lax.axis_index("batch")
    coords, subjects, verts = held.shape
    width = modes.shape[3]
    parts, rows, _ = part.shape
    own_rows = rows // n
    count, per_row, side, _ = lap.shape
    edge = tail.shape[0]
    lanes = coords * width
    share = verts // pair
    inner_blocks = count * pair
    first_row = half * count
    first = me * count * pair

    meta = [
        pltpu.make_async_copy(columns, cols, load_x.at[0]),
        pltpu.make_async_copy(table, links, load_x.at[1]),
        pltpu.make_async_copy(blocks.at[pl.ds(first_row, count)], lap, load_x.at[2]),
    ]
    mode_loads, loads = [], []
    for c in range(coords):
        mode_loads.append(
            pltpu.make_async_copy(
                modes.at[c],
                wide.at[pl.ds(0, inner_blocks), :, pl.ds(c * width, width)],
                load_m.at[c],
            )
        )
        mode_loads[-1].start()
        for j in range(parts):
            here = pl.ds(j * rows, rows)
            loads.append(
                pltpu.make_async_copy(planes.at[c, here], held.at[c, here], load_s.at[c, j])
            )
        loads[c * parts].start()
    for j in range(1, parts):
        for c in range(coords):
            loads[c * parts + j].start()
    for copy in meta:
        copy.start()

    barrier = pltpu.get_barrier_semaphore()
    for turn in range(pair):
        for step in range(n):
            if turn or step:
                pl.semaphore_signal(
                    barrier,
                    inc=1,
                    device_id={
                        "patch": lax.rem(me + step, n),
                        "batch": lax.rem(half + turn, pair),
                    },
                    device_id_type=MESH,
                )

    wide[:, :, lanes:] = jnp.ones((inner_blocks + edge, side, width), jnp.bfloat16)
    run[0] = jnp.zeros(run.shape[1:], jnp.float32)

    def modes_of(c):
        lane = slice(c * width, (c + 1) * width)
        return wide[:inner_blocks, :, lane].reshape(verts, width)

    scatters = []
    for j in range(parts):
        total = None
        for c in range(coords):
            if j == 0:
                mode_loads[c].wait()
            loads[c * parts + j].wait()
            term = dot(held[c, j * rows : (j + 1) * rows, :], modes_of(c))
            total = term if total is None else total + term
        part[j] = total
        outbox[j] = total.astype(WIRE)
        if j == 0:
            pl.semaphore_wait(barrier, n * pair - 1)
        block = []
        for step in far_first(n):
            to = lax.rem(me + step, n)
            block.append(
                pltpu.make_async_remote_copy(
                    src_ref=outbox.at[j, ds(to * own_rows, own_rows)],
                    dst_ref=land.at[j, step],
                    send_sem=send_a.at[j, step],
                    recv_sem=recv_a.at[j, step],
                    device_id={"patch": to},
                    device_id_type=MESH,
                )
            )
            block[-1].start()
        scatters.append(block)

    edge_copy = pltpu.make_async_remote_copy(
        src_ref=wide.at[pl.ds(0, edge), :, pl.ds(0, lanes)],
        dst_ref=tail,
        send_sem=edge_sem.at[0],
        recv_sem=edge_sem.at[1],
        device_id={"patch": lax.rem(me + n - 1, n), "batch": pair - 1},
        device_id_type=MESH,
    )
    gives_edge = jnp.logical_and(half == 0, me > 0)
    takes_edge = jnp.logical_and(half == pair - 1, me < n - 1)

    @pl.when(gives_edge)
    def _():
        edge_copy.start()

    @pl.when(jnp.logical_not(takes_edge))
    def _():
        tail[...] = jnp.zeros_like(tail)

    for copy in meta:
        copy.wait()
    dynamic = per_row - 1

    def block_rows(i):
        return ds(i * side, side)

    def smooth_row(i):
        mine = wide[first_row + i]
        joined = jnp.concatenate([lap[i, slot] for slot in range(per_row)], axis=1)
        targets = [
            jnp.maximum(cols[slot, first_row + i] - first, 0) for slot in range(1, per_row)
        ]
        picked = jnp.concatenate([mine] + [wide[t] for t in targets], axis=0)
        moved = lax.dot_general(joined, mine, DOWN, preferred_element_type=jnp.float32)
        acc[block_rows(i), :] = dot(joined, picked) + moved[:side]
        for slot in range(dynamic):
            before = links[slot + 1, first_row + i]
            entry = i * dynamic + slot + 1
            run[entry] = run[before] + moved[(slot + 1) * side : (slot + 2) * side]

    group = math.gcd(count - edge, 4)

    def smooth_group(outer, _):
        for inner in range(group):
            smooth_row(outer * group + inner)
        return 0

    lax.fori_loop(0, (count - edge) // group, smooth_group, 0)

    gathers = []
    for j in range(parts):
        own = ds(me * own_rows, own_rows)
        total = part[j, own, :]
        for copy, step in zip(scatters[j], far_first(n)):
            copy.wait()
            total = total + land[j, step].astype(jnp.float32)
        low[j, own, :] = (total * scale).astype(jnp.bfloat16)
        block = []
        for step in far_first(n):
            block.append(
                pltpu.make_async_remote_copy(
                    src_ref=low.at[j, own],
                    dst_ref=low.at[j, own],
                    send_sem=send_b.at[j, step],
                    recv_sem=recv_b.at[j, step],
                    device_id={"patch": lax.rem(me + step, n)},
                    device_id_type=MESH,
                )
            )
            block[-1].start()
        gathers.append(block)

    @pl.when(gives_edge)
    def _():
        edge_copy.wait_send()

    @pl.when(takes_edge)
    def _():
        edge_copy.wait_recv()

    wide[inner_blocks:, :, :lanes] = tail[...]
    for i in range(count - edge, count):
        smooth_row(i)

    carry_copy = pltpu.make_async_remote_copy(
        src_ref=carry,
        dst_ref=extra,
        send_sem=carry_sem.at[0],
        recv_sem=carry_sem.at[1],
        device_id={"patch": lax.rem(me + 1, n), "batch": 0},
        device_id_type=MESH,
    )
    gives_carry = takes_edge
    takes_carry = gives_edge
    for t in range(edge):
        sums = run[links[per_row + 1, t]]
        here = slice(t * side, (t + 1) * side)
        for c in range(coords):
            lane = slice(c * width, (c + 1) * width)
            mode = tail[t, :, lane].astype(jnp.float32)
            carry[c, here, :] = (sums[:, lanes:] * mode - sums[:, lane]).astype(jnp.bfloat16)

    @pl.when(gives_carry)
    def _():
        carry_copy.start()

    @pl.when(jnp.logical_not(takes_carry))
    def _():
        extra[...] = jnp.zeros_like(extra)

    def finish_own(i, _):
        sums = run[links[per_row, first_row + i]] + acc[block_rows(i), :]
        here = block_rows(first_row + i)
        for c in range(coords):
            lane = slice(c * width, (c + 1) * width)
            mode = wide[first_row + i, :, lane].astype(jnp.float32)
            base[c, here, :] = mode - 0.2 * (sums[:, lanes:] * mode - sums[:, lane])
        return 0

    lax.fori_loop(0, count, finish_own, 0)
    for turn in range(1, pair):
        far = lax.rem(half + turn, pair) * count

        def finish_other(i, _, far=far):
            sums = run[links[per_row, far + i]]
            here = block_rows(far + i)
            for c in range(coords):
                lane = slice(c * width, (c + 1) * width)
                mode = wide[far + i, :, lane].astype(jnp.float32)
                base[c, here, :] = -0.2 * (sums[:, lanes:] * mode - sums[:, lane])
            return 0

        lax.fori_loop(0, count, finish_other, 0)

    for c in range(coords):
        flipped[c] = modes_of(c).T

    for j in range(parts):
        for copy in gathers[j]:
            copy.wait()
        turned[:, j * rows : (j + 1) * rows] = low[j].astype(jnp.float32).T.astype(jnp.bfloat16)

    gram = lax.dot_general(turned[...], turned[...], FAR, preferred_element_type=jnp.float32)
    gram = gram * -scale
    gram_high = gram.astype(jnp.bfloat16)
    gram_low = (gram - gram_high.astype(jnp.float32)).astype(jnp.bfloat16)
    grams = jnp.concatenate([gram_high, gram_low], axis=1)
    tile = income.shape[2]
    per = share // tile

    def partial_update(c, start):
        here = ds(start, tile)
        across = flipped[c, :, here]
        hebb = dot(turned[...], held[c, :, here])
        hebb = hebb + dot(grams, jnp.concatenate([across, across], axis=0))
        return rate * hebb.T + base[c, here, :]

    exchanges = []
    for turn in range(1, pair):
        other = lax.rem(half + turn, pair)
        for k in range(coords * per):
            c, start = k // per, other * share + (k % per) * tile
            outgo[turn - 1, k] = partial_update(c, start).astype(jnp.bfloat16)
            exchanges.append(
                pltpu.make_async_remote_copy(
                    src_ref=outgo.at[turn - 1, k],
                    dst_ref=income.at[turn - 1, k],
                    send_sem=send_u.at[turn - 1, k],
                    recv_sem=recv_u.at[turn - 1, k],
                    device_id={"batch": other},
                    device_id_type=MESH,
                )
            )
            exchanges[-1].start()
    for k in range(coords * per):
        c, start = k // per, half * share + (k % per) * tile
        updated[ds(c * verts + start, tile), :] = partial_update(c, start)

    @pl.when(gives_carry)
    def _():
        carry_copy.wait_send()

    @pl.when(takes_carry)
    def _():
        carry_copy.wait_recv()

    @pl.when(half == 0)
    def _():
        for c in range(coords):
            here = pl.ds(c * verts, edge * side)
            updated[here, :] = updated[here, :] - 0.2 * extra[c].astype(jnp.float32)

    shares = []
    sums = jnp.zeros((8, width), jnp.float32)
    for k in range(coords * per):
        here = ds((k // per) * verts + half * share + (k % per) * tile, tile)
        value = updated[here, :]
        for turn in range(1, pair):
            exchanges[(turn - 1) * coords * per + k].wait()
            value = value + income[turn - 1, k].astype(jnp.float32)
        updated[here, :] = value
        sums = sums + jnp.sum((value * value).reshape(tile // 8, 8, width), axis=0)
        for turn in range(1, pair):
            shares.append(
                pltpu.make_async_remote_copy(
                    src_ref=updated.at[here],
                    dst_ref=updated.at[here],
                    send_sem=send_g.at[turn - 1, k],
                    recv_sem=recv_g.at[turn - 1, k],
                    device_id={"batch": lax.rem(half + turn, pair)},
                    device_id_type=MESH,
                )
            )
            shares[-1].start()
    mine = half * n + me
    slots[mine] = sums
    signals = []
    for turn in range(pair):
        for step in ([0] if turn else []) + far_first(n):
            at = turn * n + step
            signals.append(
                pltpu.make_async_remote_copy(
                    src_ref=slots.at[mine],
                    dst_ref=slots.at[mine],
                    send_sem=send_n.at[at],
                    recv_sem=recv_n.at[at],
                    device_id={
                        "patch": lax.rem(me + step, n),
                        "batch": lax.rem(half + turn, pair),
                    },
                    device_id_type=MESH,
                )
            )
            signals[-1].start()
    for copy in signals:
        copy.wait()
    squares = jnp.sum(jnp.sum(slots[...], axis=0), axis=0, keepdims=True)
    norms[...] = jnp.sqrt(squares / coord_count + 1e-06)
    for copy in shares:
        copy.wait()


def step(planes, modes, blocks, columns, table, scale, rate, coord_count):
    n, pair = lax.axis_size("patch"), lax.axis_size("batch")
    coords, subjects, verts = planes.shape
    width = modes.shape[2]
    all_rows, per_row, side, _ = blocks.shape
    modes = modes.reshape(coords, all_rows, side, width)
    count = all_rows // pair
    parts = max(1, min(4, subjects // (8 * n)))
    rows = subjects // parts
    reach = GHOST * side
    lanes = (coords + 1) * width
    share = verts // pair
    tile = math.gcd(share, 640)
    tiles = coords * share // tile
    dma = pltpu.SemaphoreType.DMA
    bf16, f32 = jnp.bfloat16, jnp.float32
    return pl.pallas_call(
        functools.partial(step_kernel, scale, rate, coord_count),
        out_shape=(
            jax.ShapeDtypeStruct((coords * verts, width), f32),
            jax.ShapeDtypeStruct((1, width), f32),
            jax.ShapeDtypeStruct((parts, rows, width), bf16),
        ),
        in_specs=[ANY] * 5,
        out_specs=(VMEM,) * 3,
        scratch_shapes=[
            pltpu.VMEM((coords, subjects, verts), bf16),
            pltpu.VMEM((all_rows + GHOST, side, lanes), bf16),
            pltpu.VMEM((GHOST, side, coords * width), bf16),
            pltpu.VMEM((count, per_row, side, side), bf16),
            pltpu.SMEM(columns.shape, jnp.int32),
            pltpu.SMEM(table.shape, jnp.int32),
            pltpu.VMEM((parts, rows, width), f32),
            pltpu.VMEM((parts, rows, width), WIRE),
            pltpu.VMEM((parts, n, rows // n, width), WIRE),
            pltpu.VMEM((1 + count * (per_row - 1), side, lanes), f32),
            pltpu.VMEM((count * side, lanes), f32),
            pltpu.VMEM((coords, verts, width), f32),
            pltpu.VMEM((width, subjects), bf16),
            pltpu.VMEM((coords, width, verts), bf16),
            pltpu.VMEM((pair - 1, tiles, tile, width), bf16),
            pltpu.VMEM((pair - 1, tiles, tile, width), bf16),
            pltpu.VMEM((coords, reach, width), bf16),
            pltpu.VMEM((coords, reach, width), bf16),
            pltpu.VMEM((n * pair, 8, width), f32),
            dma((coords,)),
            dma((coords, parts)),
            dma((3,)),
            dma((parts, n)),
            dma((parts, n)),
            dma((parts, n)),
            dma((parts, n)),
            dma((2,)),
            dma((2,)),
            dma((pair - 1, tiles)),
            dma((pair - 1, tiles)),
            dma((pair - 1, tiles)),
            dma((pair - 1, tiles)),
            dma((n * pair,)),
            dma((n * pair,)),
        ],
        compiler_params=pltpu.CompilerParams(
            collective_id=0, has_side_effects=True, vmem_limit_bytes=LIMIT
        ),
        name="step",
    )(planes, modes, blocks, columns, table)


def finish_kernel(updated, norm, low, out, norms, scores):
    inverse = 1.0 / norm[...]
    norms[...] = norm[...]
    scores[...] = low[...].astype(jnp.float32)
    rows = updated.shape[0]
    piece = math.gcd(rows, 256)

    def divide(i, _):
        here = ds(i * piece, piece)
        out[here, :] = (updated[here, :] * inverse).astype(jnp.bfloat16)
        return 0

    lax.fori_loop(0, rows // piece, divide, 0)


def finish(updated, norm, low):
    return pl.pallas_call(
        finish_kernel,
        out_shape=(
            jax.ShapeDtypeStruct(updated.shape, jnp.bfloat16),
            jax.ShapeDtypeStruct(norm.shape, jnp.float32),
            jax.ShapeDtypeStruct(low.shape, jnp.float32),
        ),
        in_specs=[VMEM] * 3,
        out_specs=(VMEM,) * 3,
        compiler_params=pltpu.CompilerParams(vmem_limit_bytes=16 * 1024 * 1024),
        name="finish",
    )(updated, norm, low)


def link_table(turned, first, pair, half):
    per_row, rows = turned.shape
    count = rows // pair
    slot = lax.broadcasted_iota(jnp.int32, (per_row + 2, rows), 0)
    row = lax.broadcasted_iota(jnp.int32, (per_row + 2, rows), 1)
    ends = (slot - per_row) * rows + row
    key = jnp.where(slot < per_row, jnp.pad(turned - first, ((0, 2), (0, 0))), ends)
    number = jnp.where(slot < per_row, (row - half * count) * (per_row - 1) + slot, 1 << 30)
    there = turned - first
    entry = number[:per_row]
    valid = (slot[:per_row] > 0) & (row[:per_row] // count == half)
    hits = (
        (there[:, :, None, None] == key[None, None])
        & valid[:, :, None, None]
        & (entry[:, :, None, None] < number[None, None])
    )
    return jnp.max(jnp.where(hits, entry[:, :, None, None], 0), axis=(0, 1))


def body(subjects, basis_modes, laplace_blocks, columns):
    subject_count, coords, vert_count = subjects.shape
    mode_count = basis_modes.shape[2]
    n, pair = lax.axis_size("patch"), lax.axis_size("batch")
    coord_count = coords * vert_count * n
    scale = 1.0 / math.sqrt(coord_count)
    rate = 4.0 / (subject_count * pair)
    planes = subjects.transpose(1, 0, 2)
    turned = columns.T
    first = lax.axis_index("patch") * laplace_blocks.shape[0]
    table = link_table(turned, first, pair, lax.axis_index("batch"))
    updated, norm, low = step(
        planes, basis_modes, laplace_blocks, turned, table, scale, rate, coord_count
    )
    low = low.reshape(subject_count, mode_count)
    new_modes, norms, scores = finish(updated, norm, low)
    return (scores, new_modes.reshape(coords, vert_count, mode_count), norms.reshape(mode_count))


def solution(mesh):
    placed = (
        P(("groups", "batch"), None, "patch"),
        P(None, ("groups", "patch"), None),
        P("patch", None, None, None),
        P("patch", None),
    )
    return jax.shard_map(
        body,
        mesh=mesh,
        in_specs=placed,
        out_specs=(P(("groups", "batch"), None), P(None, ("groups", "patch"), None), P("groups")),
        check_vma=False,
    )
```

```python
import functools
import math

import jax
import jax.numpy as jnp
from jax import lax
from jax.experimental import pallas as pl
from jax.experimental.pallas import tpu as pltpu
from jax.sharding import PartitionSpec as P

GHOST = 4
WIRE = jnp.bfloat16
MESH = pl.DeviceIdType.MESH
VMEM = pl.BlockSpec(memory_space=pltpu.VMEM)
ANY = pl.BlockSpec(memory_space=pl.ANY)
HBM = pl.BlockSpec(memory_space=pltpu.HBM)
LIMIT = 44 * 1024 * 1024
FAR = (((1,), (1,)), ((), ()))
DOWN = (((0,), (0,)), ((), ()))


def ds(start, size):
    return pl.ds(pl.multiple_of(start, size), size)


def far_first(n):
    return sorted(range(1, n), key=lambda step: -min(step, n - step))


def dot(a, b):
    return jnp.dot(a, b, preferred_element_type=jnp.float32)


def step_kernel(
    scale, rate, coord_count,
    planes, modes, blocks, columns,
    updated, norms, low,
    held, wide, tail, lap, cols, listed, before, last, befores, lasts, part, outbox, land, run, acc, base, turned, flipped,
    outgo, income, carry, extra, slots,
    load_m, load_s, load_x, send_a, recv_a, send_b, recv_b, edge_sem, carry_sem,
    send_u, recv_u, send_g, recv_g, send_n, recv_n,
):
    n, me = lax.axis_size("patch"), lax.axis_index("patch")
    pair, half = lax.axis_size("batch"), lax.axis_index("batch")
    coords, subjects, verts = held.shape
    width = modes.shape[3]
    parts, rows, _ = part.shape
    own_rows = rows // n
    count, per_row, side, _ = lap.shape
    edge = tail.shape[0]
    lanes = coords * width
    share = verts // pair
    inner_blocks = count * pair
    first_row = half * count
    first = me * count * pair

    meta = [
        pltpu.make_async_copy(columns, cols, load_x.at[0]),
        pltpu.make_async_copy(columns, listed, load_x.at[1]),
        pltpu.make_async_copy(blocks.at[pl.ds(first_row, count)], lap, load_x.at[2]),
    ]
    meta[0].start()
    meta[1].start()
    mode_loads, loads = [], []
    for c in range(coords):
        mode_loads.append(
            pltpu.make_async_copy(
                modes.at[c],
                wide.at[pl.ds(0, inner_blocks), :, pl.ds(c * width, width)],
                load_m.at[c],
            )
        )
        mode_loads[-1].start()
        for j in range(parts):
            here = pl.ds(j * rows, rows)
            loads.append(
                pltpu.make_async_copy(planes.at[c, here], held.at[c, here], load_s.at[c, j])
            )
        loads[c * parts].start()
    for j in range(1, parts):
        for c in range(coords):
            loads[c * parts + j].start()
    meta[2].start()

    barrier = pltpu.get_barrier_semaphore()
    for turn in range(pair):
        for step in range(n):
            if turn or step:
                pl.semaphore_signal(
                    barrier,
                    inc=1,
                    device_id={
                        "patch": lax.rem(me + step, n),
                        "batch": lax.rem(half + turn, pair),
                    },
                    device_id_type=MESH,
                )

    wide[:, :, lanes:] = jnp.ones((inner_blocks + edge, side, width), jnp.bfloat16)
    run[0] = jnp.zeros(run.shape[1:], jnp.float32)

    meta[0].wait()
    meta[1].wait()
    dynamic = per_row - 1
    slots_of = lax.broadcasted_iota(jnp.int32, listed.shape, 0)
    rows_of = lax.broadcasted_iota(jnp.int32, listed.shape, 1) - first_row
    order = rows_of * dynamic + slots_of
    wanted = listed[...] - first
    ends = lax.broadcasted_iota(jnp.int32, last.shape, 0) * inner_blocks
    ends = ends + lax.broadcasted_iota(jnp.int32, last.shape, 1)
    previous, final = jnp.zeros_like(wanted), jnp.zeros_like(ends)
    for i in range(count):
        for slot in range(1, per_row):
            entry = i * dynamic + slot
            target = cols[slot, first_row + i] - first
            previous = jnp.where((wanted == target) & (order > entry), entry, previous)
            final = jnp.where(ends == target, entry, final)
    before[...] = previous
    last[...] = final
    links = [
        pltpu.make_async_copy(before, befores, load_x.at[3]),
        pltpu.make_async_copy(last, lasts, load_x.at[4]),
    ]
    for copy in links:
        copy.start()

    def modes_of(c):
        lane = slice(c * width, (c + 1) * width)
        return wide[:inner_blocks, :, lane].reshape(verts, width)

    scatters = []
    for j in range(parts):
        total = None
        for c in range(coords):
            if j == 0:
                mode_loads[c].wait()
            loads[c * parts + j].wait()
            term = dot(held[c, j * rows : (j + 1) * rows, :], modes_of(c))
            total = term if total is None else total + term
        part[j] = total
        outbox[j] = total.astype(WIRE)
        if j == 0:
            pl.semaphore_wait(barrier, n * pair - 1)
        block = []
        for step in far_first(n):
            to = lax.rem(me + step, n)
            block.append(
                pltpu.make_async_remote_copy(
                    src_ref=outbox.at[j, ds(to * own_rows, own_rows)],
                    dst_ref=land.at[j, step],
                    send_sem=send_a.at[j, step],
                    recv_sem=recv_a.at[j, step],
                    device_id={"patch": to},
                    device_id_type=MESH,
                )
            )
            block[-1].start()
        scatters.append(block)

    edge_copy = pltpu.make_async_remote_copy(
        src_ref=wide.at[pl.ds(0, edge), :, pl.ds(0, lanes)],
        dst_ref=tail,
        send_sem=edge_sem.at[0],
        recv_sem=edge_sem.at[1],
        device_id={"patch": lax.rem(me + n - 1, n), "batch": pair - 1},
        device_id_type=MESH,
    )
    gives_edge = jnp.logical_and(half == 0, me > 0)
    takes_edge = jnp.logical_and(half == pair - 1, me < n - 1)

    @pl.when(gives_edge)
    def _():
        edge_copy.start()

    @pl.when(jnp.logical_not(takes_edge))
    def _():
        tail[...] = jnp.zeros_like(tail)

    meta[2].wait()
    for copy in links:
        copy.wait()

    def block_rows(i):
        return ds(i * side, side)

    def smooth_row(i):
        mine = wide[first_row + i]
        joined = jnp.concatenate([lap[i, slot] for slot in range(per_row)], axis=1)
        targets = [
            jnp.maximum(cols[slot, first_row + i] - first, 0) for slot in range(1, per_row)
        ]
        picked = jnp.concatenate([mine] + [wide[t] for t in targets], axis=0)
        moved = lax.dot_general(joined, mine, DOWN, preferred_element_type=jnp.float32)
        acc[block_rows(i), :] = dot(joined, picked) + moved[:side]
        for slot in range(dynamic):
            earlier = befores[slot + 1, first_row + i]
            entry = i * dynamic + slot + 1
            run[entry] = run[earlier] + moved[(slot + 1) * side : (slot + 2) * side]

    group = math.gcd(count - edge, 4)

    def smooth_group(outer, _):
        for inner in range(group):
            smooth_row(outer * group + inner)
        return 0

    lax.fori_loop(0, (count - edge) // group, smooth_group, 0)

    gathers = []
    for j in range(parts):
        own = ds(me * own_rows, own_rows)
        total = part[j, own, :]
        for copy, step in zip(scatters[j], far_first(n)):
            copy.wait()
            total = total + land[j, step].astype(jnp.float32)
        low[j, own, :] = (total * scale).astype(jnp.bfloat16)
        block = []
        for step in far_first(n):
            block.append(
                pltpu.make_async_remote_copy(
                    src_ref=low.at[j, own],
                    dst_ref=low.at[j, own],
                    send_sem=send_b.at[j, step],
                    recv_sem=recv_b.at[j, step],
                    device_id={"patch": lax.rem(me + step, n)},
                    device_id_type=MESH,
                )
            )
            block[-1].start()
        gathers.append(block)

    @pl.when(gives_edge)
    def _():
        edge_copy.wait_send()

    @pl.when(takes_edge)
    def _():
        edge_copy.wait_recv()

    wide[inner_blocks:, :, :lanes] = tail[...]
    for i in range(count - edge, count):
        smooth_row(i)

    carry_copy = pltpu.make_async_remote_copy(
        src_ref=carry,
        dst_ref=extra,
        send_sem=carry_sem.at[0],
        recv_sem=carry_sem.at[1],
        device_id={"patch": lax.rem(me + 1, n), "batch": 0},
        device_id_type=MESH,
    )
    gives_carry = takes_edge
    takes_carry = gives_edge
    for t in range(edge):
        sums = run[lasts[1, t]]
        here = slice(t * side, (t + 1) * side)
        for c in range(coords):
            lane = slice(c * width, (c + 1) * width)
            mode = tail[t, :, lane].astype(jnp.float32)
            carry[c, here, :] = (sums[:, lanes:] * mode - sums[:, lane]).astype(jnp.bfloat16)

    @pl.when(gives_carry)
    def _():
        carry_copy.start()

    @pl.when(jnp.logical_not(takes_carry))
    def _():
        extra[...] = jnp.zeros_like(extra)

    def finish_own(i, _):
        sums = run[lasts[0, first_row + i]] + acc[block_rows(i), :]
        here = block_rows(first_row + i)
        for c in range(coords):
            lane = slice(c * width, (c + 1) * width)
            mode = wide[first_row + i, :, lane].astype(jnp.float32)
            base[c, here, :] = mode - 0.2 * (sums[:, lanes:] * mode - sums[:, lane])
        return 0

    lax.fori_loop(0, count, finish_own, 0)
    for turn in range(1, pair):
        far = lax.rem(half + turn, pair) * count

        def finish_other(i, _, far=far):
            sums = run[lasts[0, far + i]]
            here = block_rows(far + i)
            for c in range(coords):
                lane = slice(c * width, (c + 1) * width)
                mode = wide[far + i, :, lane].astype(jnp.float32)
                base[c, here, :] = -0.2 * (sums[:, lanes:] * mode - sums[:, lane])
            return 0

        lax.fori_loop(0, count, finish_other, 0)

    for c in range(coords):
        flipped[c] = modes_of(c).T

    for j in range(parts):
        for copy in gathers[j]:
            copy.wait()
        turned[:, j * rows : (j + 1) * rows] = low[j].astype(jnp.float32).T.astype(jnp.bfloat16)

    gram = lax.dot_general(turned[...], turned[...], FAR, preferred_element_type=jnp.float32)
    gram = gram * -scale
    gram_high = gram.astype(jnp.bfloat16)
    gram_low = (gram - gram_high.astype(jnp.float32)).astype(jnp.bfloat16)
    grams = jnp.concatenate([gram_high, gram_low], axis=1)
    tile = income.shape[2]
    per = share // tile

    def partial_update(c, start):
        here = ds(start, tile)
        across = flipped[c, :, here]
        hebb = dot(turned[...], held[c, :, here])
        hebb = hebb + dot(grams, jnp.concatenate([across, across], axis=0))
        return rate * hebb.T + base[c, here, :]

    exchanges = []
    for turn in range(1, pair):
        other = lax.rem(half + turn, pair)
        for k in range(coords * per):
            c, start = k // per, other * share + (k % per) * tile
            outgo[turn - 1, k] = partial_update(c, start).astype(jnp.bfloat16)
            exchanges.append(
                pltpu.make_async_remote_copy(
                    src_ref=outgo.at[turn - 1, k],
                    dst_ref=income.at[turn - 1, k],
                    send_sem=send_u.at[turn - 1, k],
                    recv_sem=recv_u.at[turn - 1, k],
                    device_id={"batch": other},
                    device_id_type=MESH,
                )
            )
            exchanges[-1].start()
    for k in range(coords * per):
        c, start = k // per, half * share + (k % per) * tile
        base[c, ds(start, tile), :] = partial_update(c, start)

    @pl.when(gives_carry)
    def _():
        carry_copy.wait_send()

    @pl.when(takes_carry)
    def _():
        carry_copy.wait_recv()

    @pl.when(half == 0)
    def _():
        for c in range(coords):
            here = pl.ds(0, edge * side)
            base[c, here, :] = base[c, here, :] - 0.2 * extra[c].astype(jnp.float32)

    shares = []
    sums = jnp.zeros((8, width), jnp.float32)
    for k in range(coords * per):
        start = half * share + (k % per) * tile
        here = ds((k // per) * verts + start, tile)
        value = base[k // per, ds(start, tile), :]
        for turn in range(1, pair):
            exchanges[(turn - 1) * coords * per + k].wait()
            value = value + income[turn - 1, k].astype(jnp.float32)
        updated[here, :] = value.astype(jnp.bfloat16)
        sums = sums + jnp.sum((value * value).reshape(tile // 8, 8, width), axis=0)
        for turn in range(1, pair):
            shares.append(
                pltpu.make_async_remote_copy(
                    src_ref=updated.at[here],
                    dst_ref=updated.at[here],
                    send_sem=send_g.at[turn - 1, k],
                    recv_sem=recv_g.at[turn - 1, k],
                    device_id={"batch": lax.rem(half + turn, pair)},
                    device_id_type=MESH,
                )
            )
            shares[-1].start()
    mine = half * n + me
    slots[mine] = sums
    signals = []
    for turn in range(pair):
        for step in ([0] if turn else []) + far_first(n):
            at = turn * n + step
            signals.append(
                pltpu.make_async_remote_copy(
                    src_ref=slots.at[mine],
                    dst_ref=slots.at[mine],
                    send_sem=send_n.at[at],
                    recv_sem=recv_n.at[at],
                    device_id={
                        "patch": lax.rem(me + step, n),
                        "batch": lax.rem(half + turn, pair),
                    },
                    device_id_type=MESH,
                )
            )
            signals[-1].start()
    for copy in signals:
        copy.wait()
    squares = jnp.sum(jnp.sum(slots[...], axis=0), axis=0, keepdims=True)
    norms[...] = jnp.sqrt(squares / coord_count + 1e-06)
    for copy in shares:
        copy.wait()


def step(planes, modes, blocks, columns, scale, rate, coord_count):
    n, pair = lax.axis_size("patch"), lax.axis_size("batch")
    coords, subjects, verts = planes.shape
    width = modes.shape[2]
    all_rows, per_row, side, _ = blocks.shape
    modes = modes.reshape(coords, all_rows, side, width)
    count = all_rows // pair
    parts = max(1, min(4, subjects // (8 * n)))
    rows = subjects // parts
    reach = GHOST * side
    lanes = (coords + 1) * width
    share = verts // pair
    tile = math.gcd(share, 640)
    tiles = coords * share // tile
    dma = pltpu.SemaphoreType.DMA
    bf16, f32 = jnp.bfloat16, jnp.float32
    return pl.pallas_call(
        functools.partial(step_kernel, scale, rate, coord_count),
        out_shape=(
            jax.ShapeDtypeStruct((coords * verts, width), bf16),
            jax.ShapeDtypeStruct((1, width), f32),
            jax.ShapeDtypeStruct((parts, rows, width), bf16),
        ),
        in_specs=[HBM] * 4,
        out_specs=(VMEM,) * 3,
        scratch_shapes=[
            pltpu.VMEM((coords, subjects, verts), bf16),
            pltpu.VMEM((all_rows + GHOST, side, lanes), bf16),
            pltpu.VMEM((GHOST, side, coords * width), bf16),
            pltpu.VMEM((count, per_row, side, side), bf16),
            pltpu.SMEM(columns.shape, jnp.int32),
            pltpu.VMEM(columns.shape, jnp.int32),
            pltpu.VMEM(columns.shape, jnp.int32),
            pltpu.VMEM((2, all_rows), jnp.int32),
            pltpu.SMEM(columns.shape, jnp.int32),
            pltpu.SMEM((2, all_rows), jnp.int32),
            pltpu.VMEM((parts, rows, width), f32),
            pltpu.VMEM((parts, rows, width), WIRE),
            pltpu.VMEM((parts, n, rows // n, width), WIRE),
            pltpu.VMEM((1 + count * (per_row - 1), side, lanes), f32),
            pltpu.VMEM((count * side, lanes), f32),
            pltpu.VMEM((coords, verts, width), f32),
            pltpu.VMEM((width, subjects), bf16),
            pltpu.VMEM((coords, width, verts), bf16),
            pltpu.VMEM((pair - 1, tiles, tile, width), bf16),
            pltpu.VMEM((pair - 1, tiles, tile, width), bf16),
            pltpu.VMEM((coords, reach, width), bf16),
            pltpu.VMEM((coords, reach, width), bf16),
            pltpu.VMEM((n * pair, 8, width), f32),
            dma((coords,)),
            dma((coords, parts)),
            dma((5,)),
            dma((parts, n)),
            dma((parts, n)),
            dma((parts, n)),
            dma((parts, n)),
            dma((2,)),
            dma((2,)),
            dma((pair - 1, tiles)),
            dma((pair - 1, tiles)),
            dma((pair - 1, tiles)),
            dma((pair - 1, tiles)),
            dma((n * pair,)),
            dma((n * pair,)),
        ],
        compiler_params=pltpu.CompilerParams(
            collective_id=0, has_side_effects=True, vmem_limit_bytes=LIMIT
        ),
        name="step",
    )(*(pltpu.with_memory_space_constraint(x, pltpu.HBM) for x in (planes, modes, blocks, columns)))


def finish_kernel(updated, norm, low, out, norms, scores):
    inverse = 1.0 / norm[...]
    norms[...] = norm[...]
    scores[...] = low[...].astype(jnp.float32)
    rows = updated.shape[0]
    piece = math.gcd(rows, 256)

    def divide(i, _):
        here = ds(i * piece, piece)
        out[here, :] = (updated[here, :].astype(jnp.float32) * inverse).astype(jnp.bfloat16)
        return 0

    lax.fori_loop(0, rows // piece, divide, 0)


def finish(updated, norm, low):
    return pl.pallas_call(
        finish_kernel,
        out_shape=(
            jax.ShapeDtypeStruct(updated.shape, jnp.bfloat16),
            jax.ShapeDtypeStruct(norm.shape, jnp.float32),
            jax.ShapeDtypeStruct(low.shape, jnp.float32),
        ),
        in_specs=[VMEM] * 3,
        out_specs=(VMEM,) * 3,
        compiler_params=pltpu.CompilerParams(vmem_limit_bytes=16 * 1024 * 1024),
        name="finish",
    )(updated, norm, low)


def body(subjects, basis_modes, laplace_blocks, columns):
    subject_count, coords, vert_count = subjects.shape
    mode_count = basis_modes.shape[2]
    n, pair = lax.axis_size("patch"), lax.axis_size("batch")
    coord_count = coords * vert_count * n
    scale = 1.0 / math.sqrt(coord_count)
    rate = 4.0 / (subject_count * pair)
    planes = subjects.transpose(1, 0, 2)
    updated, norm, low = step(
        planes, basis_modes, laplace_blocks, columns.T, scale, rate, coord_count
    )
    low = low.reshape(subject_count, mode_count)
    new_modes, norms, scores = finish(updated, norm, low)
    return (scores, new_modes.reshape(coords, vert_count, mode_count), norms.reshape(mode_count))


def solution(mesh):
    placed = (
        P(("groups", "batch"), None, "patch"),
        P(None, ("groups", "patch"), None),
        P("patch", None, None, None),
        P("patch", None),
    )
    return jax.shard_map(
        body,
        mesh=mesh,
        in_specs=placed,
        out_specs=(P(("groups", "batch"), None), P(None, ("groups", "patch"), None), P("groups")),
        check_vma=False,
    )
```

```python
import functools
import math

import jax
import jax.numpy as jnp
from jax import lax
from jax.experimental import pallas as pl
from jax.experimental.pallas import tpu as pltpu
from jax.sharding import PartitionSpec as P

GHOST = 4
WIRE = jnp.bfloat16
MESH = pl.DeviceIdType.MESH
VMEM = pl.BlockSpec(memory_space=pltpu.VMEM)
ANY = pl.BlockSpec(memory_space=pl.ANY)
HBM = pl.BlockSpec(memory_space=pltpu.HBM)
LIMIT = 44 * 1024 * 1024
FAR = (((1,), (1,)), ((), ()))
DOWN = (((0,), (0,)), ((), ()))


def ds(start, size):
    return pl.ds(pl.multiple_of(start, size), size)


def far_first(n):
    return sorted(range(1, n), key=lambda step: -min(step, n - step))


def dot(a, b):
    return jnp.dot(a, b, preferred_element_type=jnp.float32)


def step_kernel(
    scale, rate, coord_count,
    planes, modes, blocks, columns,
    updated, norms, low,
    held, wide, tail, lap, cols, listed, before, last, befores, lasts, part, outbox, land, run, acc, base, turned, flipped,
    outgo, income, carry, extra, slots,
    load_m, load_s, load_x, send_a, recv_a, send_b, recv_b, edge_sem, carry_sem,
    send_u, recv_u, send_g, recv_g, send_n, recv_n,
):
    n, me = lax.axis_size("patch"), lax.axis_index("patch")
    pair, half = lax.axis_size("batch"), lax.axis_index("batch")
    coords, subjects, verts = held.shape
    width = modes.shape[3]
    parts, rows, _ = part.shape
    own_rows = rows // n
    count, per_row, side, _ = lap.shape
    edge = tail.shape[0]
    lanes = coords * width
    share = verts // pair
    inner_blocks = count * pair
    first_row = half * count
    first = me * count * pair

    meta = [
        pltpu.make_async_copy(columns, cols, load_x.at[0]),
        pltpu.make_async_copy(columns, listed, load_x.at[1]),
        pltpu.make_async_copy(blocks.at[pl.ds(first_row, count)], lap, load_x.at[2]),
    ]
    meta[0].start()
    meta[1].start()
    mode_loads, loads = [], []
    for c in range(coords):
        mode_loads.append(
            pltpu.make_async_copy(
                modes.at[c],
                wide.at[pl.ds(0, inner_blocks), :, pl.ds(c * width, width)],
                load_m.at[c],
            )
        )
        mode_loads[-1].start()
        for j in range(parts):
            here = pl.ds(j * rows, rows)
            loads.append(
                pltpu.make_async_copy(planes.at[c, here], held.at[c, here], load_s.at[c, j])
            )
        loads[c * parts].start()
    for j in range(1, parts):
        for c in range(coords):
            loads[c * parts + j].start()
    meta[2].start()

    barrier = pltpu.get_barrier_semaphore()
    for turn in range(pair):
        for step in range(n):
            if turn or step:
                pl.semaphore_signal(
                    barrier,
                    inc=1,
                    device_id={
                        "patch": lax.rem(me + step, n),
                        "batch": lax.rem(half + turn, pair),
                    },
                    device_id_type=MESH,
                )

    wide[:, :, lanes:] = jnp.ones((inner_blocks + edge, side, width), jnp.bfloat16)
    run[0] = jnp.zeros(run.shape[1:], jnp.float32)

    meta[0].wait()
    meta[1].wait()
    dynamic = per_row - 1
    slots_of = lax.broadcasted_iota(jnp.int32, listed.shape, 0)
    rows_of = lax.broadcasted_iota(jnp.int32, listed.shape, 1) - first_row
    order = rows_of * dynamic + slots_of
    wanted = listed[...] - first
    ends = lax.broadcasted_iota(jnp.int32, last.shape, 0) * inner_blocks
    ends = ends + lax.broadcasted_iota(jnp.int32, last.shape, 1)
    previous, final = jnp.zeros_like(wanted), jnp.zeros_like(ends)
    for i in range(count):
        for slot in range(1, per_row):
            entry = i * dynamic + slot
            target = cols[slot, first_row + i] - first
            previous = jnp.where((wanted == target) & (order > entry), entry, previous)
            final = jnp.where(ends == target, entry, final)
    before[...] = previous
    last[...] = final
    links = [
        pltpu.make_async_copy(before, befores, load_x.at[3]),
        pltpu.make_async_copy(last, lasts, load_x.at[4]),
    ]
    for copy in links:
        copy.start()

    def modes_of(c):
        lane = slice(c * width, (c + 1) * width)
        return wide[:inner_blocks, :, lane].reshape(verts, width)

    scatters = []
    for j in range(parts):
        total = None
        for c in range(coords):
            if j == 0:
                mode_loads[c].wait()
            loads[c * parts + j].wait()
            term = dot(held[c, j * rows : (j + 1) * rows, :], modes_of(c))
            total = term if total is None else total + term
        part[j] = total
        outbox[j] = total.astype(WIRE)
        if j == 0:
            pl.semaphore_wait(barrier, n * pair - 1)
        block = []
        for step in far_first(n):
            to = lax.rem(me + step, n)
            block.append(
                pltpu.make_async_remote_copy(
                    src_ref=outbox.at[j, ds(to * own_rows, own_rows)],
                    dst_ref=land.at[j, step],
                    send_sem=send_a.at[j, step],
                    recv_sem=recv_a.at[j, step],
                    device_id={"patch": to},
                    device_id_type=MESH,
                )
            )
            block[-1].start()
        scatters.append(block)

    edge_copy = pltpu.make_async_remote_copy(
        src_ref=wide.at[pl.ds(0, edge), :, pl.ds(0, lanes)],
        dst_ref=tail,
        send_sem=edge_sem.at[0],
        recv_sem=edge_sem.at[1],
        device_id={"patch": lax.rem(me + n - 1, n), "batch": pair - 1},
        device_id_type=MESH,
    )
    gives_edge = jnp.logical_and(half == 0, me > 0)
    takes_edge = jnp.logical_and(half == pair - 1, me < n - 1)

    @pl.when(gives_edge)
    def _():
        edge_copy.start()

    @pl.when(jnp.logical_not(takes_edge))
    def _():
        tail[...] = jnp.zeros_like(tail)

    meta[2].wait()
    for copy in links:
        copy.wait()

    def block_rows(i):
        return ds(i * side, side)

    def smooth_row(i):
        mine = wide[first_row + i]
        joined = jnp.concatenate([lap[i, slot] for slot in range(per_row)], axis=1)
        targets = [
            jnp.maximum(cols[slot, first_row + i] - first, 0) for slot in range(1, per_row)
        ]
        picked = jnp.concatenate([mine] + [wide[t] for t in targets], axis=0)
        moved = lax.dot_general(joined, mine, DOWN, preferred_element_type=jnp.float32)
        acc[block_rows(i), :] = dot(joined, picked) + moved[:side]
        for slot in range(dynamic):
            earlier = befores[slot + 1, first_row + i]
            entry = i * dynamic + slot + 1
            run[entry] = run[earlier] + moved[(slot + 1) * side : (slot + 2) * side]

    group = math.gcd(count - edge, 4)

    def smooth_group(outer, _):
        for inner in range(group):
            smooth_row(outer * group + inner)
        return 0

    lax.fori_loop(0, (count - edge) // group, smooth_group, 0)

    gathers = []
    for j in range(parts):
        own = ds(me * own_rows, own_rows)
        total = part[j, own, :]
        for copy, step in zip(scatters[j], far_first(n)):
            copy.wait()
            total = total + land[j, step].astype(jnp.float32)
        low[j, own, :] = (total * scale).astype(jnp.bfloat16)
        block = []
        for step in far_first(n):
            block.append(
                pltpu.make_async_remote_copy(
                    src_ref=low.at[j, own],
                    dst_ref=low.at[j, own],
                    send_sem=send_b.at[j, step],
                    recv_sem=recv_b.at[j, step],
                    device_id={"patch": lax.rem(me + step, n)},
                    device_id_type=MESH,
                )
            )
            block[-1].start()
        gathers.append(block)

    @pl.when(gives_edge)
    def _():
        edge_copy.wait_send()

    @pl.when(takes_edge)
    def _():
        edge_copy.wait_recv()

    wide[inner_blocks:, :, :lanes] = tail[...]
    for i in range(count - edge, count):
        smooth_row(i)

    carry_copy = pltpu.make_async_remote_copy(
        src_ref=carry,
        dst_ref=extra,
        send_sem=carry_sem.at[0],
        recv_sem=carry_sem.at[1],
        device_id={"patch": lax.rem(me + 1, n), "batch": 0},
        device_id_type=MESH,
    )
    gives_carry = takes_edge
    takes_carry = gives_edge
    for t in range(edge):
        sums = run[lasts[1, t]]
        here = slice(t * side, (t + 1) * side)
        for c in range(coords):
            lane = slice(c * width, (c + 1) * width)
            mode = tail[t, :, lane].astype(jnp.float32)
            carry[c, here, :] = (sums[:, lanes:] * mode - sums[:, lane]).astype(jnp.bfloat16)

    @pl.when(gives_carry)
    def _():
        carry_copy.start()

    @pl.when(jnp.logical_not(takes_carry))
    def _():
        extra[...] = jnp.zeros_like(extra)

    def finish_own(i, _):
        sums = run[lasts[0, first_row + i]] + acc[block_rows(i), :]
        here = block_rows(first_row + i)
        for c in range(coords):
            lane = slice(c * width, (c + 1) * width)
            mode = wide[first_row + i, :, lane].astype(jnp.float32)
            base[c, here, :] = mode - 0.2 * (sums[:, lanes:] * mode - sums[:, lane])
        return 0

    lax.fori_loop(0, count, finish_own, 0)
    for turn in range(1, pair):
        far = lax.rem(half + turn, pair) * count

        def finish_other(i, _, far=far):
            sums = run[lasts[0, far + i]]
            here = block_rows(far + i)
            for c in range(coords):
                lane = slice(c * width, (c + 1) * width)
                mode = wide[far + i, :, lane].astype(jnp.float32)
                base[c, here, :] = -0.2 * (sums[:, lanes:] * mode - sums[:, lane])
            return 0

        lax.fori_loop(0, count, finish_other, 0)

    for c in range(coords):
        flipped[c] = modes_of(c).T

    tile = income.shape[2]
    per = share // tile

    def arrive(blocks_of):
        for j in blocks_of:
            for copy in gathers[j]:
                copy.wait()
            turned[:, j * rows : (j + 1) * rows] = (
                low[j].astype(jnp.float32).T.astype(jnp.bfloat16)
            )
        span = slice(blocks_of[0] * rows, (blocks_of[-1] + 1) * rows)
        front = turned[:, span]
        gram = lax.dot_general(front, front, FAR, preferred_element_type=jnp.float32)
        gram = gram * -scale
        high = gram.astype(jnp.bfloat16)
        rest = (gram - high.astype(jnp.float32)).astype(jnp.bfloat16)
        grams = jnp.concatenate([high, rest], axis=1)

        def partial_update(c, start):
            here = ds(start, tile)
            across = flipped[c, :, here]
            hebb = dot(front, held[c, span, here])
            hebb = hebb + dot(grams, jnp.concatenate([across, across], axis=0))
            return rate * hebb.T + base[c, here, :]

        return partial_update

    early = parts // 2
    if early:
        partial_update = arrive(list(range(early)))
        for k in range(coords * verts // tile):
            c, start = k * tile // verts, k * tile % verts
            base[c, start : start + tile, :] = partial_update(c, start)
    partial_update = arrive(list(range(early, parts)))

    exchanges = []
    for turn in range(1, pair):
        other = lax.rem(half + turn, pair)
        for k in range(coords * per):
            c, start = k // per, other * share + (k % per) * tile
            outgo[turn - 1, k] = partial_update(c, start).astype(jnp.bfloat16)
            exchanges.append(
                pltpu.make_async_remote_copy(
                    src_ref=outgo.at[turn - 1, k],
                    dst_ref=income.at[turn - 1, k],
                    send_sem=send_u.at[turn - 1, k],
                    recv_sem=recv_u.at[turn - 1, k],
                    device_id={"batch": other},
                    device_id_type=MESH,
                )
            )
            exchanges[-1].start()
    for k in range(coords * per):
        c, start = k // per, half * share + (k % per) * tile
        base[c, ds(start, tile), :] = partial_update(c, start)

    @pl.when(gives_carry)
    def _():
        carry_copy.wait_send()

    @pl.when(takes_carry)
    def _():
        carry_copy.wait_recv()

    @pl.when(half == 0)
    def _():
        for c in range(coords):
            here = pl.ds(0, edge * side)
            base[c, here, :] = base[c, here, :] - 0.2 * extra[c].astype(jnp.float32)

    shares = []
    sums = jnp.zeros((8, width), jnp.float32)
    for k in range(coords * per):
        start = half * share + (k % per) * tile
        here = ds((k // per) * verts + start, tile)
        value = base[k // per, ds(start, tile), :]
        for turn in range(1, pair):
            exchanges[(turn - 1) * coords * per + k].wait()
            value = value + income[turn - 1, k].astype(jnp.float32)
        updated[here, :] = value.astype(jnp.bfloat16)
        sums = sums + jnp.sum((value * value).reshape(tile // 8, 8, width), axis=0)
        for turn in range(1, pair):
            shares.append(
                pltpu.make_async_remote_copy(
                    src_ref=updated.at[here],
                    dst_ref=updated.at[here],
                    send_sem=send_g.at[turn - 1, k],
                    recv_sem=recv_g.at[turn - 1, k],
                    device_id={"batch": lax.rem(half + turn, pair)},
                    device_id_type=MESH,
                )
            )
            shares[-1].start()
    mine = half * n + me
    slots[mine] = jnp.sum(sums, axis=0, keepdims=True)
    signals = []
    for turn in range(pair):
        for step in ([0] if turn else []) + far_first(n):
            at = turn * n + step
            signals.append(
                pltpu.make_async_remote_copy(
                    src_ref=slots.at[mine],
                    dst_ref=slots.at[mine],
                    send_sem=send_n.at[at],
                    recv_sem=recv_n.at[at],
                    device_id={
                        "patch": lax.rem(me + step, n),
                        "batch": lax.rem(half + turn, pair),
                    },
                    device_id_type=MESH,
                )
            )
            signals[-1].start()
    for copy in signals:
        copy.wait()
    squares = jnp.sum(slots[...], axis=0)
    norms[...] = jnp.sqrt(squares / coord_count + 1e-06)
    for copy in shares:
        copy.wait()


def step(planes, modes, blocks, columns, scale, rate, coord_count):
    n, pair = lax.axis_size("patch"), lax.axis_size("batch")
    coords, subjects, verts = planes.shape
    width = modes.shape[2]
    all_rows, per_row, side, _ = blocks.shape
    modes = modes.reshape(coords, all_rows, side, width)
    count = all_rows // pair
    parts = max(1, min(4, subjects // (8 * n)))
    rows = subjects // parts
    reach = GHOST * side
    lanes = (coords + 1) * width
    share = verts // pair
    tile = math.gcd(share, 640)
    tiles = coords * share // tile
    dma = pltpu.SemaphoreType.DMA
    bf16, f32 = jnp.bfloat16, jnp.float32
    return pl.pallas_call(
        functools.partial(step_kernel, scale, rate, coord_count),
        out_shape=(
            jax.ShapeDtypeStruct((coords * verts, width), bf16),
            jax.ShapeDtypeStruct((1, width), f32),
            jax.ShapeDtypeStruct((parts, rows, width), bf16),
        ),
        in_specs=[HBM] * 4,
        out_specs=(VMEM,) * 3,
        scratch_shapes=[
            pltpu.VMEM((coords, subjects, verts), bf16),
            pltpu.VMEM((all_rows + GHOST, side, lanes), bf16),
            pltpu.VMEM((GHOST, side, coords * width), bf16),
            pltpu.VMEM((count, per_row, side, side), bf16),
            pltpu.SMEM(columns.shape, jnp.int32),
            pltpu.VMEM(columns.shape, jnp.int32),
            pltpu.VMEM(columns.shape, jnp.int32),
            pltpu.VMEM((2, all_rows), jnp.int32),
            pltpu.SMEM(columns.shape, jnp.int32),
            pltpu.SMEM((2, all_rows), jnp.int32),
            pltpu.VMEM((parts, rows, width), f32),
            pltpu.VMEM((parts, rows, width), WIRE),
            pltpu.VMEM((parts, n, rows // n, width), WIRE),
            pltpu.VMEM((1 + count * (per_row - 1), side, lanes), f32),
            pltpu.VMEM((count * side, lanes), f32),
            pltpu.VMEM((coords, verts, width), f32),
            pltpu.VMEM((width, subjects), bf16),
            pltpu.VMEM((coords, width, verts), bf16),
            pltpu.VMEM((pair - 1, tiles, tile, width), bf16),
            pltpu.VMEM((pair - 1, tiles, tile, width), bf16),
            pltpu.VMEM((coords, reach, width), bf16),
            pltpu.VMEM((coords, reach, width), bf16),
            pltpu.VMEM((n * pair, 1, width), f32),
            dma((coords,)),
            dma((coords, parts)),
            dma((5,)),
            dma((parts, n)),
            dma((parts, n)),
            dma((parts, n)),
            dma((parts, n)),
            dma((2,)),
            dma((2,)),
            dma((pair - 1, tiles)),
            dma((pair - 1, tiles)),
            dma((pair - 1, tiles)),
            dma((pair - 1, tiles)),
            dma((n * pair,)),
            dma((n * pair,)),
        ],
        compiler_params=pltpu.CompilerParams(
            collective_id=0, has_side_effects=True, vmem_limit_bytes=LIMIT
        ),
        name="step",
    )(*(pltpu.with_memory_space_constraint(x, pltpu.HBM) for x in (planes, modes, blocks, columns)))


def finish_kernel(updated, norm, low, out, norms, scores, held, wide, sems):
    inverse = 1.0 / norm[...]
    norms[...] = norm[...]
    pieces, rows, _ = held.shape
    wide[...] = low[...].astype(jnp.float32)
    copies = [pltpu.make_async_copy(wide, scores, sems.at[pieces])]
    copies[0].start()
    piece = math.gcd(rows, 128)
    for k in range(pieces):

        def divide(i, _, k=k):
            value = updated[ds(k * rows + i * piece, piece), :].astype(jnp.float32)
            held[k, ds(i * piece, piece), :] = (value * inverse).astype(jnp.bfloat16)
            return 0

        lax.fori_loop(0, rows // piece, divide, 0)
        copies.append(pltpu.make_async_copy(held.at[k], out.at[pl.ds(k * rows, rows)], sems.at[k]))
        copies[-1].start()
    for copy in copies:
        copy.wait()


def finish(updated, norm, low):
    rows, width = updated.shape
    pieces = 6
    return pl.pallas_call(
        finish_kernel,
        out_shape=(
            jax.ShapeDtypeStruct(updated.shape, jnp.bfloat16),
            jax.ShapeDtypeStruct(norm.shape, jnp.float32),
            jax.ShapeDtypeStruct(low.shape, jnp.float32),
        ),
        in_specs=[VMEM] * 3,
        out_specs=(ANY, VMEM, ANY),
        scratch_shapes=[
            pltpu.VMEM((pieces, rows // pieces, width), jnp.bfloat16),
            pltpu.VMEM(low.shape, jnp.float32),
            pltpu.SemaphoreType.DMA((pieces + 1,)),
        ],
        compiler_params=pltpu.CompilerParams(vmem_limit_bytes=16 * 1024 * 1024),
        name="finish",
    )(updated, norm, low)


def body(subjects, basis_modes, laplace_blocks, columns):
    subject_count, coords, vert_count = subjects.shape
    mode_count = basis_modes.shape[2]
    n, pair = lax.axis_size("patch"), lax.axis_size("batch")
    coord_count = coords * vert_count * n
    scale = 1.0 / math.sqrt(coord_count)
    rate = 4.0 / (subject_count * pair)
    planes = subjects.transpose(1, 0, 2)
    updated, norm, low = step(
        planes, basis_modes, laplace_blocks, columns.T, scale, rate, coord_count
    )
    low = low.reshape(subject_count, mode_count)
    new_modes, norms, scores = finish(updated, norm, low)
    return (scores, new_modes.reshape(coords, vert_count, mode_count), norms.reshape(mode_count))


def solution(mesh):
    placed = (
        P(("groups", "batch"), None, "patch"),
        P(None, ("groups", "patch"), None),
        P("patch", None, None, None),
        P("patch", None),
    )
    return jax.shard_map(
        body,
        mesh=mesh,
        in_specs=placed,
        out_specs=(P(("groups", "batch"), None), P(None, ("groups", "patch"), None), P("groups")),
        check_vma=False,
    )
```

```python
import functools
import math

import jax
import jax.numpy as jnp
from jax import lax
from jax.experimental import pallas as pl
from jax.experimental.pallas import tpu as pltpu
from jax.sharding import PartitionSpec as P

GHOST = 4
WIRE = jnp.bfloat16
MESH = pl.DeviceIdType.MESH
VMEM = pl.BlockSpec(memory_space=pltpu.VMEM)
ANY = pl.BlockSpec(memory_space=pl.ANY)
HBM = pl.BlockSpec(memory_space=pltpu.HBM)
LIMIT = 44 * 1024 * 1024
FAR = (((1,), (1,)), ((), ()))
DOWN = (((0,), (0,)), ((), ()))


def ds(start, size):
    return pl.ds(pl.multiple_of(start, size), size)


def eights(start, size):
    return pl.ds(pl.multiple_of(start, 8), size)


def far_first(n):
    return sorted(range(1, n), key=lambda step: -min(step, n - step))


def dot(a, b):
    return jnp.dot(a, b, preferred_element_type=jnp.float32)


def step_kernel(
    sizes, scale, rate, coord_count,
    planes, modes, blocks, columns,
    updated, norms, low,
    held, wide, tail, lap, cols, listed, before, last, befores, lasts, part, outbox, land, run, acc, base, turned, flipped,
    outgo, income, carry, extra, slots,
    load_m, load_s, load_x, send_a, recv_a, send_b, recv_b, edge_sem, carry_sem,
    send_u, recv_u, send_g, recv_g, send_n, recv_n,
):
    n, me = lax.axis_size("patch"), lax.axis_index("patch")
    pair, half = lax.axis_size("batch"), lax.axis_index("batch")
    coords, subjects, verts = held.shape
    width = modes.shape[3]
    parts = len(sizes)
    starts = [sum(sizes[:j]) for j in range(parts)]
    count, per_row, side, _ = lap.shape
    edge = tail.shape[0]
    lanes = coords * width
    share = verts // pair
    inner_blocks = count * pair
    first_row = half * count
    first = me * count * pair

    meta = [
        pltpu.make_async_copy(columns, cols, load_x.at[0]),
        pltpu.make_async_copy(columns, listed, load_x.at[1]),
        pltpu.make_async_copy(blocks.at[pl.ds(first_row, count)], lap, load_x.at[2]),
    ]
    meta[0].start()
    meta[1].start()
    mode_loads, loads = [], []
    for c in range(coords):
        mode_loads.append(
            pltpu.make_async_copy(
                modes.at[c],
                wide.at[pl.ds(0, inner_blocks), :, pl.ds(c * width, width)],
                load_m.at[c],
            )
        )
        mode_loads[-1].start()
        for j in range(parts):
            here = pl.ds(starts[j], sizes[j])
            loads.append(
                pltpu.make_async_copy(planes.at[c, here], held.at[c, here], load_s.at[c, j])
            )
        loads[c * parts].start()
    for j in range(1, parts):
        for c in range(coords):
            loads[c * parts + j].start()
    meta[2].start()

    barrier = pltpu.get_barrier_semaphore()
    for turn in range(pair):
        for step in range(n):
            if turn or step:
                pl.semaphore_signal(
                    barrier,
                    inc=1,
                    device_id={
                        "patch": lax.rem(me + step, n),
                        "batch": lax.rem(half + turn, pair),
                    },
                    device_id_type=MESH,
                )

    wide[:, :, lanes:] = jnp.ones((inner_blocks + edge, side, width), jnp.bfloat16)
    run[0] = jnp.zeros(run.shape[1:], jnp.float32)

    meta[0].wait()
    meta[1].wait()
    dynamic = per_row - 1
    slots_of = lax.broadcasted_iota(jnp.int32, listed.shape, 0)
    rows_of = lax.broadcasted_iota(jnp.int32, listed.shape, 1) - first_row
    order = rows_of * dynamic + slots_of
    wanted = listed[...] - first
    ends = lax.broadcasted_iota(jnp.int32, last.shape, 0) * inner_blocks
    ends = ends + lax.broadcasted_iota(jnp.int32, last.shape, 1)
    previous, final = jnp.zeros_like(wanted), jnp.zeros_like(ends)
    for i in range(count):
        for slot in range(1, per_row):
            entry = i * dynamic + slot
            target = cols[slot, first_row + i] - first
            previous = jnp.where((wanted == target) & (order > entry), entry, previous)
            final = jnp.where(ends == target, entry, final)
    before[...] = previous
    last[...] = final
    links = [
        pltpu.make_async_copy(before, befores, load_x.at[3]),
        pltpu.make_async_copy(last, lasts, load_x.at[4]),
    ]
    for copy in links:
        copy.start()

    def modes_of(c):
        lane = slice(c * width, (c + 1) * width)
        return wide[:inner_blocks, :, lane].reshape(verts, width)

    scatters = []
    for j in range(parts):
        total = None
        block_of = slice(starts[j], starts[j] + sizes[j])
        own_rows = sizes[j] // n
        for c in range(coords):
            if j == 0:
                mode_loads[c].wait()
            loads[c * parts + j].wait()
            term = dot(held[c, block_of, :], modes_of(c))
            total = term if total is None else total + term
        part[block_of, :] = total
        outbox[block_of, :] = total.astype(WIRE)
        if j == 0:
            pl.semaphore_wait(barrier, n * pair - 1)
        block = []
        for step in far_first(n):
            to = lax.rem(me + step, n)
            block.append(
                pltpu.make_async_remote_copy(
                    src_ref=outbox.at[eights(starts[j] + to * own_rows, own_rows)],
                    dst_ref=land.at[step, pl.ds(starts[j] // n, own_rows)],
                    send_sem=send_a.at[j, step],
                    recv_sem=recv_a.at[j, step],
                    device_id={"patch": to},
                    device_id_type=MESH,
                )
            )
            block[-1].start()
        scatters.append(block)

    edge_copy = pltpu.make_async_remote_copy(
        src_ref=wide.at[pl.ds(0, edge), :, pl.ds(0, lanes)],
        dst_ref=tail,
        send_sem=edge_sem.at[0],
        recv_sem=edge_sem.at[1],
        device_id={"patch": lax.rem(me + n - 1, n), "batch": pair - 1},
        device_id_type=MESH,
    )
    gives_edge = jnp.logical_and(half == 0, me > 0)
    takes_edge = jnp.logical_and(half == pair - 1, me < n - 1)

    @pl.when(gives_edge)
    def _():
        edge_copy.start()

    @pl.when(jnp.logical_not(takes_edge))
    def _():
        tail[...] = jnp.zeros_like(tail)

    meta[2].wait()
    for copy in links:
        copy.wait()

    def block_rows(i):
        return ds(i * side, side)

    def smooth_row(i):
        mine = wide[first_row + i]
        joined = jnp.concatenate([lap[i, slot] for slot in range(per_row)], axis=1)
        targets = [
            jnp.maximum(cols[slot, first_row + i] - first, 0) for slot in range(1, per_row)
        ]
        picked = jnp.concatenate([mine] + [wide[t] for t in targets], axis=0)
        moved = lax.dot_general(joined, mine, DOWN, preferred_element_type=jnp.float32)
        acc[block_rows(i), :] = dot(joined, picked) + moved[:side]
        for slot in range(dynamic):
            earlier = befores[slot + 1, first_row + i]
            entry = i * dynamic + slot + 1
            run[entry] = run[earlier] + moved[(slot + 1) * side : (slot + 2) * side]

    group = math.gcd(count - edge, 4)

    def smooth_group(outer, _):
        for inner in range(group):
            smooth_row(outer * group + inner)
        return 0

    lax.fori_loop(0, (count - edge) // group, smooth_group, 0)

    gathers = []
    for j in range(parts):
        own_rows = sizes[j] // n
        own = eights(starts[j] + me * own_rows, own_rows)
        total = part[own, :]
        for copy, step in zip(scatters[j], far_first(n)):
            copy.wait()
            landed = slice(starts[j] // n, starts[j] // n + own_rows)
            total = total + land[step, landed, :].astype(jnp.float32)
        low[own, :] = (total * scale).astype(jnp.bfloat16)
        block = []
        for step in far_first(n):
            block.append(
                pltpu.make_async_remote_copy(
                    src_ref=low.at[own],
                    dst_ref=low.at[own],
                    send_sem=send_b.at[j, step],
                    recv_sem=recv_b.at[j, step],
                    device_id={"patch": lax.rem(me + step, n)},
                    device_id_type=MESH,
                )
            )
            block[-1].start()
        gathers.append(block)

    @pl.when(gives_edge)
    def _():
        edge_copy.wait_send()

    @pl.when(takes_edge)
    def _():
        edge_copy.wait_recv()

    wide[inner_blocks:, :, :lanes] = tail[...]
    for i in range(count - edge, count):
        smooth_row(i)

    carry_copy = pltpu.make_async_remote_copy(
        src_ref=carry,
        dst_ref=extra,
        send_sem=carry_sem.at[0],
        recv_sem=carry_sem.at[1],
        device_id={"patch": lax.rem(me + 1, n), "batch": 0},
        device_id_type=MESH,
    )
    gives_carry = takes_edge
    takes_carry = gives_edge
    for t in range(edge):
        sums = run[lasts[1, t]]
        here = slice(t * side, (t + 1) * side)
        for c in range(coords):
            lane = slice(c * width, (c + 1) * width)
            mode = tail[t, :, lane].astype(jnp.float32)
            carry[c, here, :] = (sums[:, lanes:] * mode - sums[:, lane]).astype(jnp.bfloat16)

    @pl.when(gives_carry)
    def _():
        carry_copy.start()

    @pl.when(jnp.logical_not(takes_carry))
    def _():
        extra[...] = jnp.zeros_like(extra)

    def finish_own(i, _):
        sums = run[lasts[0, first_row + i]] + acc[block_rows(i), :]
        here = block_rows(first_row + i)
        for c in range(coords):
            lane = slice(c * width, (c + 1) * width)
            mode = wide[first_row + i, :, lane].astype(jnp.float32)
            base[c, here, :] = mode - 0.2 * (sums[:, lanes:] * mode - sums[:, lane])
        return 0

    lax.fori_loop(0, count, finish_own, 0)
    for turn in range(1, pair):
        far = lax.rem(half + turn, pair) * count

        def finish_other(i, _, far=far):
            sums = run[lasts[0, far + i]]
            here = block_rows(far + i)
            for c in range(coords):
                lane = slice(c * width, (c + 1) * width)
                mode = wide[far + i, :, lane].astype(jnp.float32)
                base[c, here, :] = -0.2 * (sums[:, lanes:] * mode - sums[:, lane])
            return 0

        lax.fori_loop(0, count, finish_other, 0)

    for c in range(coords):
        flipped[c] = modes_of(c).T

    tile = income.shape[2]
    per = share // tile

    def arrive(blocks_of):
        for j in blocks_of:
            for copy in gathers[j]:
                copy.wait()
        span = slice(starts[blocks_of[0]], starts[blocks_of[-1]] + sizes[blocks_of[-1]])
        turned[:, span] = low[span, :].astype(jnp.float32).T.astype(jnp.bfloat16)
        front = turned[:, span]
        gram = lax.dot_general(front, front, FAR, preferred_element_type=jnp.float32)
        gram = gram * -scale
        high = gram.astype(jnp.bfloat16)
        rest = (gram - high.astype(jnp.float32)).astype(jnp.bfloat16)
        grams = jnp.concatenate([high, rest], axis=1)

        def partial_update(c, start):
            here = ds(start, tile)
            across = flipped[c, :, here]
            hebb = dot(front, held[c, span, here])
            hebb = hebb + dot(grams, jnp.concatenate([across, across], axis=0))
            return rate * hebb.T + base[c, here, :]

        return partial_update

    early = parts // 2
    if early:
        partial_update = arrive(list(range(early)))
        for k in range(coords * verts // tile):
            c, start = k * tile // verts, k * tile % verts
            base[c, start : start + tile, :] = partial_update(c, start)
    partial_update = arrive(list(range(early, parts)))

    exchanges = []
    for turn in range(1, pair):
        other = lax.rem(half + turn, pair)
        for k in range(coords * per):
            c, start = k // per, other * share + (k % per) * tile
            outgo[turn - 1, k] = partial_update(c, start).astype(jnp.bfloat16)
            exchanges.append(
                pltpu.make_async_remote_copy(
                    src_ref=outgo.at[turn - 1, k],
                    dst_ref=income.at[turn - 1, k],
                    send_sem=send_u.at[turn - 1, k],
                    recv_sem=recv_u.at[turn - 1, k],
                    device_id={"batch": other},
                    device_id_type=MESH,
                )
            )
            exchanges[-1].start()
    for k in range(coords * per):
        c, start = k // per, half * share + (k % per) * tile
        base[c, ds(start, tile), :] = partial_update(c, start)

    @pl.when(gives_carry)
    def _():
        carry_copy.wait_send()

    @pl.when(takes_carry)
    def _():
        carry_copy.wait_recv()

    @pl.when(half == 0)
    def _():
        for c in range(coords):
            here = pl.ds(0, edge * side)
            base[c, here, :] = base[c, here, :] - 0.2 * extra[c].astype(jnp.float32)

    shares = []
    sums = jnp.zeros((8, width), jnp.float32)
    for k in range(coords * per):
        start = half * share + (k % per) * tile
        here = ds((k // per) * verts + start, tile)
        value = base[k // per, ds(start, tile), :]
        for turn in range(1, pair):
            exchanges[(turn - 1) * coords * per + k].wait()
            value = value + income[turn - 1, k].astype(jnp.float32)
        updated[here, :] = value.astype(jnp.bfloat16)
        sums = sums + jnp.sum((value * value).reshape(tile // 8, 8, width), axis=0)
        for turn in range(1, pair):
            shares.append(
                pltpu.make_async_remote_copy(
                    src_ref=updated.at[here],
                    dst_ref=updated.at[here],
                    send_sem=send_g.at[turn - 1, k],
                    recv_sem=recv_g.at[turn - 1, k],
                    device_id={"batch": lax.rem(half + turn, pair)},
                    device_id_type=MESH,
                )
            )
            shares[-1].start()
    mine = half * n + me
    slots[mine] = jnp.sum(sums, axis=0, keepdims=True)
    signals = []
    for turn in range(pair):
        for step in ([0] if turn else []) + far_first(n):
            at = turn * n + step
            signals.append(
                pltpu.make_async_remote_copy(
                    src_ref=slots.at[mine],
                    dst_ref=slots.at[mine],
                    send_sem=send_n.at[at],
                    recv_sem=recv_n.at[at],
                    device_id={
                        "patch": lax.rem(me + step, n),
                        "batch": lax.rem(half + turn, pair),
                    },
                    device_id_type=MESH,
                )
            )
            signals[-1].start()
    for copy in signals:
        copy.wait()
    squares = jnp.sum(slots[...], axis=0)
    norms[...] = jnp.sqrt(squares / coord_count + 1e-06)
    for copy in shares:
        copy.wait()


def step(planes, modes, blocks, columns, scale, rate, coord_count):
    n, pair = lax.axis_size("patch"), lax.axis_size("batch")
    coords, subjects, verts = planes.shape
    width = modes.shape[2]
    all_rows, per_row, side, _ = blocks.shape
    modes = modes.reshape(coords, all_rows, side, width)
    count = all_rows // pair
    parts = max(1, min(4, subjects // (8 * n)))
    sizes = [subjects // parts] * parts
    if parts == 4 and subjects % (64 * n) == 0:
        sizes = [subjects // 8 * units for units in (2, 2, 3, 1)]
    reach = GHOST * side
    lanes = (coords + 1) * width
    share = verts // pair
    tile = math.gcd(share, 640)
    tiles = coords * share // tile
    dma = pltpu.SemaphoreType.DMA
    bf16, f32 = jnp.bfloat16, jnp.float32
    return pl.pallas_call(
        functools.partial(step_kernel, sizes, scale, rate, coord_count),
        out_shape=(
            jax.ShapeDtypeStruct((coords * verts, width), bf16),
            jax.ShapeDtypeStruct((1, width), f32),
            jax.ShapeDtypeStruct((subjects, width), bf16),
        ),
        in_specs=[HBM] * 4,
        out_specs=(VMEM,) * 3,
        scratch_shapes=[
            pltpu.VMEM((coords, subjects, verts), bf16),
            pltpu.VMEM((all_rows + GHOST, side, lanes), bf16),
            pltpu.VMEM((GHOST, side, coords * width), bf16),
            pltpu.VMEM((count, per_row, side, side), bf16),
            pltpu.SMEM(columns.shape, jnp.int32),
            pltpu.VMEM(columns.shape, jnp.int32),
            pltpu.VMEM(columns.shape, jnp.int32),
            pltpu.VMEM((2, all_rows), jnp.int32),
            pltpu.SMEM(columns.shape, jnp.int32),
            pltpu.SMEM((2, all_rows), jnp.int32),
            pltpu.VMEM((subjects, width), f32),
            pltpu.VMEM((subjects, width), WIRE),
            pltpu.VMEM((n, subjects // n, width), WIRE),
            pltpu.VMEM((1 + count * (per_row - 1), side, lanes), f32),
            pltpu.VMEM((count * side, lanes), f32),
            pltpu.VMEM((coords, verts, width), f32),
            pltpu.VMEM((width, subjects), bf16),
            pltpu.VMEM((coords, width, verts), bf16),
            pltpu.VMEM((pair - 1, tiles, tile, width), bf16),
            pltpu.VMEM((pair - 1, tiles, tile, width), bf16),
            pltpu.VMEM((coords, reach, width), bf16),
            pltpu.VMEM((coords, reach, width), bf16),
            pltpu.VMEM((n * pair, 1, width), f32),
            dma((coords,)),
            dma((coords, parts)),
            dma((5,)),
            dma((parts, n)),
            dma((parts, n)),
            dma((parts, n)),
            dma((parts, n)),
            dma((2,)),
            dma((2,)),
            dma((pair - 1, tiles)),
            dma((pair - 1, tiles)),
            dma((pair - 1, tiles)),
            dma((pair - 1, tiles)),
            dma((n * pair,)),
            dma((n * pair,)),
        ],
        compiler_params=pltpu.CompilerParams(
            collective_id=0, has_side_effects=True, vmem_limit_bytes=LIMIT
        ),
        name="step",
    )(*(pltpu.with_memory_space_constraint(x, pltpu.HBM) for x in (planes, modes, blocks, columns)))


def finish_kernel(updated, norm, low, out, norms, scores, held, wide, sems):
    inverse = 1.0 / norm[...]
    norms[...] = norm[...]
    pieces, rows, _ = held.shape
    wide[...] = low[...].astype(jnp.float32)
    copies = [pltpu.make_async_copy(wide, scores, sems.at[pieces])]
    copies[0].start()
    for k in range(pieces):
        value = updated[k * rows : (k + 1) * rows, :].astype(jnp.float32)
        held[k] = (value * inverse).astype(jnp.bfloat16)
        copies.append(pltpu.make_async_copy(held.at[k], out.at[pl.ds(k * rows, rows)], sems.at[k]))
        copies[-1].start()
    for copy in copies:
        copy.wait()


def finish(updated, norm, low):
    rows, width = updated.shape
    pieces = 6
    return pl.pallas_call(
        finish_kernel,
        out_shape=(
            jax.ShapeDtypeStruct(updated.shape, jnp.bfloat16),
            jax.ShapeDtypeStruct(norm.shape, jnp.float32),
            jax.ShapeDtypeStruct(low.shape, jnp.float32),
        ),
        in_specs=[VMEM] * 3,
        out_specs=(ANY, VMEM, ANY),
        scratch_shapes=[
            pltpu.VMEM((pieces, rows // pieces, width), jnp.bfloat16),
            pltpu.VMEM(low.shape, jnp.float32),
            pltpu.SemaphoreType.DMA((pieces + 1,)),
        ],
        compiler_params=pltpu.CompilerParams(vmem_limit_bytes=16 * 1024 * 1024),
        name="finish",
    )(updated, norm, low)


def body(subjects, basis_modes, laplace_blocks, columns):
    subject_count, coords, vert_count = subjects.shape
    mode_count = basis_modes.shape[2]
    n, pair = lax.axis_size("patch"), lax.axis_size("batch")
    coord_count = coords * vert_count * n
    scale = 1.0 / math.sqrt(coord_count)
    rate = 4.0 / (subject_count * pair)
    planes = subjects.transpose(1, 0, 2)
    updated, norm, low = step(
        planes, basis_modes, laplace_blocks, columns.T, scale, rate, coord_count
    )
    new_modes, norms, scores = finish(updated, norm, low)
    return (scores, new_modes.reshape(coords, vert_count, mode_count), norms.reshape(mode_count))


def solution(mesh):
    placed = (
        P(("groups", "batch"), None, "patch"),
        P(None, ("groups", "patch"), None),
        P("patch", None, None, None),
        P("patch", None),
    )
    return jax.shard_map(
        body,
        mesh=mesh,
        in_specs=placed,
        out_specs=(P(("groups", "batch"), None), P(None, ("groups", "patch"), None), P("groups")),
        check_vma=False,
    )
```

```python
import functools
import math

import jax
import jax.numpy as jnp
from jax import lax
from jax.experimental import pallas as pl
from jax.experimental.pallas import tpu as pltpu
from jax.sharding import PartitionSpec as P

GHOST = 4
WIRE = jnp.bfloat16
MESH = pl.DeviceIdType.MESH
VMEM = pl.BlockSpec(memory_space=pltpu.VMEM)
ANY = pl.BlockSpec(memory_space=pl.ANY)
HBM = pl.BlockSpec(memory_space=pltpu.HBM)
LIMIT = 44 * 1024 * 1024
FAR = (((1,), (1,)), ((), ()))
DOWN = (((0,), (0,)), ((), ()))


def ds(start, size):
    return pl.ds(pl.multiple_of(start, size), size)


def eights(start, size):
    return pl.ds(pl.multiple_of(start, 8), size)


def far_first(n):
    return sorted(range(1, n), key=lambda step: -min(step, n - step))


def dot(a, b):
    return jnp.dot(a, b, preferred_element_type=jnp.float32)


def step_kernel(
    sizes, scale, rate, coord_count,
    planes, modes, blocks, columns,
    updated, norms, low,
    held, wide, tail, lap, cols, listed, before, last, befores, lasts, part, outbox, land, run, acc, base, turned, flipped,
    outgo, income, carry, extra, slots,
    load_m, load_s, load_x, send_a, recv_a, send_b, recv_b, edge_sem, carry_sem,
    send_u, recv_u, send_g, recv_g, send_n, recv_n,
):
    n, me = lax.axis_size("patch"), lax.axis_index("patch")
    pair, half = lax.axis_size("batch"), lax.axis_index("batch")
    coords, subjects, verts = held.shape
    width = modes.shape[3]
    parts = len(sizes)
    starts = [sum(sizes[:j]) for j in range(parts)]
    count, per_row, side, _ = lap.shape
    edge = tail.shape[0]
    lanes = coords * width
    share = verts // pair
    inner_blocks = count * pair
    first_row = half * count
    first = me * count * pair

    meta = [
        pltpu.make_async_copy(columns, cols, load_x.at[0]),
        pltpu.make_async_copy(columns, listed, load_x.at[1]),
        pltpu.make_async_copy(blocks.at[pl.ds(first_row, count)], lap, load_x.at[2]),
    ]
    meta[0].start()
    meta[1].start()
    mode_loads, loads = [], []
    for c in range(coords):
        mode_loads.append(
            pltpu.make_async_copy(
                modes.at[c],
                wide.at[pl.ds(0, inner_blocks), :, pl.ds(c * width, width)],
                load_m.at[c],
            )
        )
        mode_loads[-1].start()
        for j in range(parts):
            here = pl.ds(starts[j], sizes[j])
            loads.append(
                pltpu.make_async_copy(planes.at[c, here], held.at[c, here], load_s.at[c, j])
            )
        loads[c * parts].start()
    for j in range(1, parts):
        for c in range(coords):
            loads[c * parts + j].start()
    meta[2].start()

    barrier = pltpu.get_barrier_semaphore()
    for turn in range(pair):
        for step in range(n):
            if turn or step:
                pl.semaphore_signal(
                    barrier,
                    inc=1,
                    device_id={
                        "patch": lax.rem(me + step, n),
                        "batch": lax.rem(half + turn, pair),
                    },
                    device_id_type=MESH,
                )

    wide[:, :, lanes:] = jnp.ones((inner_blocks + edge, side, width), jnp.bfloat16)
    run[0] = jnp.zeros(run.shape[1:], jnp.float32)

    meta[0].wait()
    meta[1].wait()
    dynamic = per_row - 1
    slots_of = lax.broadcasted_iota(jnp.int32, listed.shape, 0)
    rows_of = lax.broadcasted_iota(jnp.int32, listed.shape, 1) - first_row
    order = rows_of * dynamic + slots_of
    wanted = listed[...] - first
    ends = lax.broadcasted_iota(jnp.int32, last.shape, 0) * inner_blocks
    ends = ends + lax.broadcasted_iota(jnp.int32, last.shape, 1)
    previous, final = jnp.zeros_like(wanted), jnp.zeros_like(ends)
    for i in range(count):
        for slot in range(1, per_row):
            entry = i * dynamic + slot
            target = cols[slot, first_row + i] - first
            previous = jnp.where((wanted == target) & (order > entry), entry, previous)
            final = jnp.where(ends == target, entry, final)
    before[...] = previous
    last[...] = final
    links = [
        pltpu.make_async_copy(before, befores, load_x.at[3]),
        pltpu.make_async_copy(last, lasts, load_x.at[4]),
    ]
    for copy in links:
        copy.start()

    def modes_of(c):
        lane = slice(c * width, (c + 1) * width)
        return wide[:inner_blocks, :, lane].reshape(verts, width)

    scatters = []
    for j in range(parts):
        total = None
        block_of = slice(starts[j], starts[j] + sizes[j])
        own_rows = sizes[j] // n
        for c in range(coords):
            if j == 0:
                mode_loads[c].wait()
            loads[c * parts + j].wait()
            term = dot(held[c, block_of, :], modes_of(c))
            total = term if total is None else total + term
        part[block_of, :] = total
        outbox[block_of, :] = total.astype(WIRE)
        if j == 0:
            pl.semaphore_wait(barrier, n * pair - 1)
        block = []
        for step in far_first(n):
            to = lax.rem(me + step, n)
            block.append(
                pltpu.make_async_remote_copy(
                    src_ref=outbox.at[eights(starts[j] + to * own_rows, own_rows)],
                    dst_ref=land.at[step, pl.ds(starts[j] // n, own_rows)],
                    send_sem=send_a.at[j, step],
                    recv_sem=recv_a.at[j, step],
                    device_id={"patch": to},
                    device_id_type=MESH,
                )
            )
            block[-1].start()
        scatters.append(block)

    edge_copy = pltpu.make_async_remote_copy(
        src_ref=wide.at[pl.ds(0, edge), :, pl.ds(0, lanes)],
        dst_ref=tail,
        send_sem=edge_sem.at[0],
        recv_sem=edge_sem.at[1],
        device_id={"patch": lax.rem(me + n - 1, n), "batch": pair - 1},
        device_id_type=MESH,
    )
    gives_edge = jnp.logical_and(half == 0, me > 0)
    takes_edge = jnp.logical_and(half == pair - 1, me < n - 1)

    @pl.when(gives_edge)
    def _():
        edge_copy.start()

    @pl.when(jnp.logical_not(takes_edge))
    def _():
        tail[...] = jnp.zeros_like(tail)

    meta[2].wait()
    for copy in links:
        copy.wait()

    def block_rows(i):
        return ds(i * side, side)

    def smooth_row(i):
        mine = wide[first_row + i]
        joined = jnp.concatenate([lap[i, slot] for slot in range(per_row)], axis=1)
        targets = [
            jnp.maximum(cols[slot, first_row + i] - first, 0) for slot in range(1, per_row)
        ]
        picked = jnp.concatenate([mine] + [wide[t] for t in targets], axis=0)
        moved = lax.dot_general(joined, mine, DOWN, preferred_element_type=jnp.float32)
        acc[block_rows(i), :] = dot(joined, picked) + moved[:side]
        for slot in range(dynamic):
            earlier = befores[slot + 1, first_row + i]
            entry = i * dynamic + slot + 1
            run[entry] = run[earlier] + moved[(slot + 1) * side : (slot + 2) * side]

    group = math.gcd(count - edge, 4)

    def smooth_group(outer, _):
        for inner in range(group):
            smooth_row(outer * group + inner)
        return 0

    lax.fori_loop(0, (count - edge) // group, smooth_group, 0)

    gathers = []
    for j in range(parts):
        own_rows = sizes[j] // n
        own = eights(starts[j] + me * own_rows, own_rows)
        total = part[own, :]
        for copy, step in zip(scatters[j], far_first(n)):
            copy.wait()
            landed = slice(starts[j] // n, starts[j] // n + own_rows)
            total = total + land[step, landed, :].astype(jnp.float32)
        low[own, :] = (total * scale).astype(jnp.bfloat16)
        block = []
        for step in far_first(n):
            block.append(
                pltpu.make_async_remote_copy(
                    src_ref=low.at[own],
                    dst_ref=low.at[own],
                    send_sem=send_b.at[j, step],
                    recv_sem=recv_b.at[j, step],
                    device_id={"patch": lax.rem(me + step, n)},
                    device_id_type=MESH,
                )
            )
            block[-1].start()
        gathers.append(block)

    @pl.when(gives_edge)
    def _():
        edge_copy.wait_send()

    @pl.when(takes_edge)
    def _():
        edge_copy.wait_recv()

    wide[inner_blocks:, :, :lanes] = tail[...]
    for i in range(count - edge, count):
        smooth_row(i)

    carry_copy = pltpu.make_async_remote_copy(
        src_ref=carry,
        dst_ref=extra,
        send_sem=carry_sem.at[0],
        recv_sem=carry_sem.at[1],
        device_id={"patch": lax.rem(me + 1, n), "batch": 0},
        device_id_type=MESH,
    )
    gives_carry = takes_edge
    takes_carry = gives_edge
    for t in range(edge):
        sums = run[lasts[1, t]]
        here = slice(t * side, (t + 1) * side)
        for c in range(coords):
            lane = slice(c * width, (c + 1) * width)
            mode = tail[t, :, lane].astype(jnp.float32)
            carry[c, here, :] = (sums[:, lanes:] * mode - sums[:, lane]).astype(jnp.bfloat16)

    @pl.when(gives_carry)
    def _():
        carry_copy.start()

    @pl.when(jnp.logical_not(takes_carry))
    def _():
        extra[...] = jnp.zeros_like(extra)

    def finish_own(i, _):
        sums = run[lasts[0, first_row + i]] + acc[block_rows(i), :]
        here = block_rows(first_row + i)
        for c in range(coords):
            lane = slice(c * width, (c + 1) * width)
            mode = wide[first_row + i, :, lane].astype(jnp.float32)
            base[c, here, :] = mode - 0.2 * (sums[:, lanes:] * mode - sums[:, lane])
        return 0

    lax.fori_loop(0, count, finish_own, 0)
    for turn in range(1, pair):
        far = lax.rem(half + turn, pair) * count

        def finish_other(i, _, far=far):
            sums = run[lasts[0, far + i]]
            here = block_rows(far + i)
            for c in range(coords):
                lane = slice(c * width, (c + 1) * width)
                mode = wide[far + i, :, lane].astype(jnp.float32)
                base[c, here, :] = -0.2 * (sums[:, lanes:] * mode - sums[:, lane])
            return 0

        lax.fori_loop(0, count, finish_other, 0)

    for c in range(coords):
        flipped[c] = modes_of(c).T

    tile = income.shape[2]
    per = share // tile

    def arrive(blocks_of):
        for j in blocks_of:
            for copy in gathers[j]:
                copy.wait()
        span = slice(starts[blocks_of[0]], starts[blocks_of[-1]] + sizes[blocks_of[-1]])
        turned[:, span] = low[span, :].astype(jnp.float32).T.astype(jnp.bfloat16)
        front = turned[:, span]
        gram = lax.dot_general(front, front, FAR, preferred_element_type=jnp.float32)
        gram = gram * -scale
        high = gram.astype(jnp.bfloat16)
        rest = (gram - high.astype(jnp.float32)).astype(jnp.bfloat16)
        grams = jnp.concatenate([high, rest], axis=1)

        def partial_update(c, start):
            here = ds(start, tile)
            across = flipped[c, :, here]
            hebb = dot(front, held[c, span, here])
            hebb = hebb + dot(grams, jnp.concatenate([across, across], axis=0))
            return rate * hebb.T + base[c, here, :]

        return partial_update

    early = parts // 2
    if early:
        partial_update = arrive(list(range(early)))
        for k in range(coords * verts // tile):
            c, start = k * tile // verts, k * tile % verts
            base[c, start : start + tile, :] = partial_update(c, start)
    partial_update = arrive(list(range(early, parts)))

    exchanges = []
    for turn in range(1, pair):
        other = lax.rem(half + turn, pair)
        for k in range(coords * per):
            c, start = k // per, other * share + (k % per) * tile
            outgo[turn - 1, k] = partial_update(c, start).astype(jnp.bfloat16)
            exchanges.append(
                pltpu.make_async_remote_copy(
                    src_ref=outgo.at[turn - 1, k],
                    dst_ref=income.at[turn - 1, k],
                    send_sem=send_u.at[turn - 1, k],
                    recv_sem=recv_u.at[turn - 1, k],
                    device_id={"batch": other},
                    device_id_type=MESH,
                )
            )
            exchanges[-1].start()
    for k in range(coords * per):
        c, start = k // per, half * share + (k % per) * tile
        base[c, ds(start, tile), :] = partial_update(c, start)

    @pl.when(gives_carry)
    def _():
        carry_copy.wait_send()

    @pl.when(takes_carry)
    def _():
        carry_copy.wait_recv()

    @pl.when(half == 0)
    def _():
        for c in range(coords):
            here = pl.ds(0, edge * side)
            base[c, here, :] = base[c, here, :] - 0.2 * extra[c].astype(jnp.float32)

    shares = []
    sums = jnp.zeros((8, width), jnp.float32)
    for k in range(coords * per):
        start = half * share + (k % per) * tile
        here = ds((k // per) * verts + start, tile)
        value = base[k // per, ds(start, tile), :]
        for turn in range(1, pair):
            exchanges[(turn - 1) * coords * per + k].wait()
            value = value + income[turn - 1, k].astype(jnp.float32)
        updated[here, :] = value.astype(jnp.bfloat16)
        sums = sums + jnp.sum((value * value).reshape(tile // 8, 8, width), axis=0)
        for turn in range(1, pair):
            shares.append(
                pltpu.make_async_remote_copy(
                    src_ref=updated.at[here],
                    dst_ref=updated.at[here],
                    send_sem=send_g.at[turn - 1, k],
                    recv_sem=recv_g.at[turn - 1, k],
                    device_id={"batch": lax.rem(half + turn, pair)},
                    device_id_type=MESH,
                )
            )
            shares[-1].start()
    mine = half * n + me
    slots[mine] = jnp.sum(sums, axis=0, keepdims=True)
    signals = []
    for turn in range(pair):
        for step in ([0] if turn else []) + far_first(n):
            at = turn * n + step
            signals.append(
                pltpu.make_async_remote_copy(
                    src_ref=slots.at[mine],
                    dst_ref=slots.at[mine],
                    send_sem=send_n.at[at],
                    recv_sem=recv_n.at[at],
                    device_id={
                        "patch": lax.rem(me + step, n),
                        "batch": lax.rem(half + turn, pair),
                    },
                    device_id_type=MESH,
                )
            )
            signals[-1].start()
    for copy in signals:
        copy.wait()
    squares = jnp.sum(slots[...], axis=0)
    norms[...] = jnp.sqrt(squares / coord_count + 1e-06)
    for copy in shares:
        copy.wait()


def step(planes, modes, blocks, columns, scale, rate, coord_count):
    n, pair = lax.axis_size("patch"), lax.axis_size("batch")
    coords, subjects, verts = planes.shape
    width = modes.shape[2]
    all_rows, per_row, side, _ = blocks.shape
    modes = modes.reshape(coords, all_rows, side, width)
    count = all_rows // pair
    parts = max(1, min(4, subjects // (8 * n)))
    sizes = [subjects // parts] * parts
    if parts == 4 and subjects % (64 * n) == 0:
        sizes = [subjects // 8 * units for units in (2, 2, 3, 1)]
    reach = GHOST * side
    lanes = (coords + 1) * width
    share = verts // pair
    tile = math.gcd(share, 256)
    tiles = coords * share // tile
    dma = pltpu.SemaphoreType.DMA
    bf16, f32 = jnp.bfloat16, jnp.float32
    return pl.pallas_call(
        functools.partial(step_kernel, sizes, scale, rate, coord_count),
        out_shape=(
            jax.ShapeDtypeStruct((coords * verts, width), bf16),
            jax.ShapeDtypeStruct((1, width), f32),
            jax.ShapeDtypeStruct((subjects, width), bf16),
        ),
        in_specs=[HBM] * 4,
        out_specs=(VMEM,) * 3,
        scratch_shapes=[
            pltpu.VMEM((coords, subjects, verts), bf16),
            pltpu.VMEM((all_rows + GHOST, side, lanes), bf16),
            pltpu.VMEM((GHOST, side, coords * width), bf16),
            pltpu.VMEM((count, per_row, side, side), bf16),
            pltpu.SMEM(columns.shape, jnp.int32),
            pltpu.VMEM(columns.shape, jnp.int32),
            pltpu.VMEM(columns.shape, jnp.int32),
            pltpu.VMEM((2, all_rows), jnp.int32),
            pltpu.SMEM(columns.shape, jnp.int32),
            pltpu.SMEM((2, all_rows), jnp.int32),
            pltpu.VMEM((subjects, width), f32),
            pltpu.VMEM((subjects, width), WIRE),
            pltpu.VMEM((n, subjects // n, width), WIRE),
            pltpu.VMEM((1 + count * (per_row - 1), side, lanes), f32),
            pltpu.VMEM((count * side, lanes), f32),
            pltpu.VMEM((coords, verts, width), f32),
            pltpu.VMEM((width, subjects), bf16),
            pltpu.VMEM((coords, width, verts), bf16),
            pltpu.VMEM((pair - 1, tiles, tile, width), bf16),
            pltpu.VMEM((pair - 1, tiles, tile, width), bf16),
            pltpu.VMEM((coords, reach, width), bf16),
            pltpu.VMEM((coords, reach, width), bf16),
            pltpu.VMEM((n * pair, 1, width), f32),
            dma((coords,)),
            dma((coords, parts)),
            dma((5,)),
            dma((parts, n)),
            dma((parts, n)),
            dma((parts, n)),
            dma((parts, n)),
            dma((2,)),
            dma((2,)),
            dma((pair - 1, tiles)),
            dma((pair - 1, tiles)),
            dma((pair - 1, tiles)),
            dma((pair - 1, tiles)),
            dma((n * pair,)),
            dma((n * pair,)),
        ],
        compiler_params=pltpu.CompilerParams(
            collective_id=0, has_side_effects=True, vmem_limit_bytes=LIMIT
        ),
        name="step",
    )(*(pltpu.with_memory_space_constraint(x, pltpu.HBM) for x in (planes, modes, blocks, columns)))


def finish_kernel(updated, norm, low, out, norms, scores, held, wide, sems):
    inverse = 1.0 / norm[...]
    norms[...] = norm[...]
    pieces, rows, _ = held.shape
    wide[...] = low[...].astype(jnp.float32)
    copies = [pltpu.make_async_copy(wide, scores, sems.at[pieces])]
    copies[0].start()
    for k in range(pieces):
        value = updated[k * rows : (k + 1) * rows, :].astype(jnp.float32)
        held[k] = (value * inverse).astype(jnp.bfloat16)
        copies.append(pltpu.make_async_copy(held.at[k], out.at[pl.ds(k * rows, rows)], sems.at[k]))
        copies[-1].start()
    for copy in copies:
        copy.wait()


def finish(updated, norm, low):
    rows, width = updated.shape
    pieces = 6
    return pl.pallas_call(
        finish_kernel,
        out_shape=(
            jax.ShapeDtypeStruct(updated.shape, jnp.bfloat16),
            jax.ShapeDtypeStruct(norm.shape, jnp.float32),
            jax.ShapeDtypeStruct(low.shape, jnp.float32),
        ),
        in_specs=[VMEM] * 3,
        out_specs=(ANY, VMEM, ANY),
        scratch_shapes=[
            pltpu.VMEM((pieces, rows // pieces, width), jnp.bfloat16),
            pltpu.VMEM(low.shape, jnp.float32),
            pltpu.SemaphoreType.DMA((pieces + 1,)),
        ],
        compiler_params=pltpu.CompilerParams(vmem_limit_bytes=16 * 1024 * 1024),
        name="finish",
    )(updated, norm, low)


def body(subjects, basis_modes, laplace_blocks, columns):
    subject_count, coords, vert_count = subjects.shape
    mode_count = basis_modes.shape[2]
    n, pair = lax.axis_size("patch"), lax.axis_size("batch")
    coord_count = coords * vert_count * n
    scale = 1.0 / math.sqrt(coord_count)
    rate = 4.0 / (subject_count * pair)
    planes = subjects.transpose(1, 0, 2)
    updated, norm, low = step(
        planes, basis_modes, laplace_blocks, columns.T, scale, rate, coord_count
    )
    new_modes, norms, scores = finish(updated, norm, low)
    return (scores, new_modes.reshape(coords, vert_count, mode_count), norms.reshape(mode_count))


def solution(mesh):
    placed = (
        P(("groups", "batch"), None, "patch"),
        P(None, ("groups", "patch"), None),
        P("patch", None, None, None),
        P("patch", None),
    )
    return jax.shard_map(
        body,
        mesh=mesh,
        in_specs=placed,
        out_specs=(P(("groups", "batch"), None), P(None, ("groups", "patch"), None), P("groups")),
        check_vma=False,
    )
```

```python
import functools
import math

import jax
import jax.numpy as jnp
from jax import lax
from jax.experimental import pallas as pl
from jax.experimental.pallas import tpu as pltpu
from jax.sharding import PartitionSpec as P

GHOST = 4
WIRE = jnp.bfloat16
MESH = pl.DeviceIdType.MESH
VMEM = pl.BlockSpec(memory_space=pltpu.VMEM)
ANY = pl.BlockSpec(memory_space=pl.ANY)
HBM = pl.BlockSpec(memory_space=pltpu.HBM)
LIMIT = 44 * 1024 * 1024
FAR = (((1,), (1,)), ((), ()))
DOWN = (((0,), (0,)), ((), ()))


def ds(start, size):
    return pl.ds(pl.multiple_of(start, size), size)


def eights(start, size):
    return pl.ds(pl.multiple_of(start, 8), size)


def far_first(n):
    return sorted(range(1, n), key=lambda step: -min(step, n - step))


def dot(a, b):
    return jnp.dot(a, b, preferred_element_type=jnp.float32)


def step_kernel(
    sizes, scale, rate, coord_count,
    planes, modes, blocks, columns,
    updated, norms, low,
    held, wide, tail, lap, cols, listed, before, last, befores, lasts, part, outbox, land, run, acc, base, turned, flipped,
    outgo, income, carry, extra, slots,
    load_m, load_s, load_x, send_a, recv_a, send_b, recv_b, edge_sem, carry_sem,
    send_u, recv_u, send_g, recv_g, send_n, recv_n,
):
    n, me = lax.axis_size("patch"), lax.axis_index("patch")
    pair, half = lax.axis_size("batch"), lax.axis_index("batch")
    coords, subjects, verts = held.shape
    width = modes.shape[3]
    parts = len(sizes)
    starts = [sum(sizes[:j]) for j in range(parts)]
    count, per_row, side, _ = lap.shape
    edge = tail.shape[0]
    lanes = coords * width
    share = verts // pair
    inner_blocks = count * pair
    first_row = half * count
    first = me * count * pair

    meta = [
        pltpu.make_async_copy(columns, cols, load_x.at[0]),
        pltpu.make_async_copy(columns, listed, load_x.at[1]),
        pltpu.make_async_copy(blocks.at[pl.ds(first_row, count)], lap, load_x.at[2]),
    ]
    meta[0].start()
    meta[1].start()
    mode_loads, loads = [], []
    for c in range(coords):
        mode_loads.append(
            pltpu.make_async_copy(
                modes.at[c],
                wide.at[pl.ds(0, inner_blocks), :, pl.ds(c * width, width)],
                load_m.at[c],
            )
        )
        mode_loads[-1].start()
        for j in range(parts):
            here = pl.ds(starts[j], sizes[j])
            loads.append(
                pltpu.make_async_copy(planes.at[c, here], held.at[c, here], load_s.at[c, j])
            )
        loads[c * parts].start()
    for j in range(1, parts):
        for c in range(coords):
            loads[c * parts + j].start()
    meta[2].start()

    barrier = pltpu.get_barrier_semaphore()
    for turn in range(pair):
        for step in range(n):
            if turn or step:
                pl.semaphore_signal(
                    barrier,
                    inc=1,
                    device_id={
                        "patch": lax.rem(me + step, n),
                        "batch": lax.rem(half + turn, pair),
                    },
                    device_id_type=MESH,
                )

    wide[:, :, lanes:] = jnp.ones((inner_blocks + edge, side, width), jnp.bfloat16)
    run[0] = jnp.zeros(run.shape[1:], jnp.float32)

    meta[0].wait()
    meta[1].wait()
    dynamic = per_row - 1
    slots_of = lax.broadcasted_iota(jnp.int32, listed.shape, 0)
    rows_of = lax.broadcasted_iota(jnp.int32, listed.shape, 1) - first_row
    order = rows_of * dynamic + slots_of
    wanted = listed[...] - first
    ends = lax.broadcasted_iota(jnp.int32, last.shape, 0) * inner_blocks
    ends = ends + lax.broadcasted_iota(jnp.int32, last.shape, 1)
    previous, final = jnp.zeros_like(wanted), jnp.zeros_like(ends)
    for i in range(count):
        for slot in range(1, per_row):
            entry = i * dynamic + slot
            target = cols[slot, first_row + i] - first
            previous = jnp.where((wanted == target) & (order > entry), entry, previous)
            final = jnp.where(ends == target, entry, final)
    before[...] = previous
    last[...] = final
    links = [
        pltpu.make_async_copy(before, befores, load_x.at[3]),
        pltpu.make_async_copy(last, lasts, load_x.at[4]),
    ]
    for copy in links:
        copy.start()

    def modes_of(c):
        lane = slice(c * width, (c + 1) * width)
        return wide[:inner_blocks, :, lane].reshape(verts, width)

    scatters = []
    for j in range(parts):
        total = None
        block_of = slice(starts[j], starts[j] + sizes[j])
        own_rows = sizes[j] // n
        for c in range(coords):
            if j == 0:
                mode_loads[c].wait()
            loads[c * parts + j].wait()
            term = dot(held[c, block_of, :], modes_of(c))
            total = term if total is None else total + term
        part[block_of, :] = total
        outbox[block_of, :] = total.astype(WIRE)
        if j == 0:
            pl.semaphore_wait(barrier, n * pair - 1)
        block = []
        for step in far_first(n):
            to = lax.rem(me + step, n)
            block.append(
                pltpu.make_async_remote_copy(
                    src_ref=outbox.at[eights(starts[j] + to * own_rows, own_rows)],
                    dst_ref=land.at[step, pl.ds(starts[j] // n, own_rows)],
                    send_sem=send_a.at[j, step],
                    recv_sem=recv_a.at[j, step],
                    device_id={"patch": to},
                    device_id_type=MESH,
                )
            )
            block[-1].start()
        scatters.append(block)

    edge_copy = pltpu.make_async_remote_copy(
        src_ref=wide.at[pl.ds(0, edge), :, pl.ds(0, lanes)],
        dst_ref=tail,
        send_sem=edge_sem.at[0],
        recv_sem=edge_sem.at[1],
        device_id={"patch": lax.rem(me + n - 1, n), "batch": pair - 1},
        device_id_type=MESH,
    )
    gives_edge = jnp.logical_and(half == 0, me > 0)
    takes_edge = jnp.logical_and(half == pair - 1, me < n - 1)

    @pl.when(gives_edge)
    def _():
        edge_copy.start()

    @pl.when(jnp.logical_not(takes_edge))
    def _():
        tail[...] = jnp.zeros_like(tail)

    meta[2].wait()
    for copy in links:
        copy.wait()

    def block_rows(i):
        return ds(i * side, side)

    def smooth_row(i):
        mine = wide[first_row + i]
        joined = jnp.concatenate([lap[i, slot] for slot in range(per_row)], axis=1)
        targets = [
            jnp.maximum(cols[slot, first_row + i] - first, 0) for slot in range(1, per_row)
        ]
        picked = jnp.concatenate([mine] + [wide[t] for t in targets], axis=0)
        moved = lax.dot_general(joined, mine, DOWN, preferred_element_type=jnp.float32)
        acc[block_rows(i), :] = dot(joined, picked) + moved[:side]
        for slot in range(dynamic):
            earlier = befores[slot + 1, first_row + i]
            entry = i * dynamic + slot + 1
            run[entry] = run[earlier] + moved[(slot + 1) * side : (slot + 2) * side]

    group = math.gcd(count - edge, 4)

    def smooth_group(outer, _):
        for inner in range(group):
            smooth_row(outer * group + inner)
        return 0

    lax.fori_loop(0, (count - edge) // group, smooth_group, 0)

    gathers = []
    for j in range(parts):
        own_rows = sizes[j] // n
        own = eights(starts[j] + me * own_rows, own_rows)
        total = part[own, :]
        for copy, step in zip(scatters[j], far_first(n)):
            copy.wait()
            landed = slice(starts[j] // n, starts[j] // n + own_rows)
            total = total + land[step, landed, :].astype(jnp.float32)
        low[own, :] = (total * scale).astype(jnp.bfloat16)
        block = []
        for step in far_first(n):
            block.append(
                pltpu.make_async_remote_copy(
                    src_ref=low.at[own],
                    dst_ref=low.at[own],
                    send_sem=send_b.at[j, step],
                    recv_sem=recv_b.at[j, step],
                    device_id={"patch": lax.rem(me + step, n)},
                    device_id_type=MESH,
                )
            )
            block[-1].start()
        gathers.append(block)

    @pl.when(gives_edge)
    def _():
        edge_copy.wait_send()

    @pl.when(takes_edge)
    def _():
        edge_copy.wait_recv()

    wide[inner_blocks:, :, :lanes] = tail[...]
    for i in range(count - edge, count):
        smooth_row(i)

    carry_copy = pltpu.make_async_remote_copy(
        src_ref=carry,
        dst_ref=extra,
        send_sem=carry_sem.at[0],
        recv_sem=carry_sem.at[1],
        device_id={"patch": lax.rem(me + 1, n), "batch": 0},
        device_id_type=MESH,
    )
    gives_carry = takes_edge
    takes_carry = gives_edge
    for t in range(edge):
        sums = run[lasts[1, t]]
        here = slice(t * side, (t + 1) * side)
        for c in range(coords):
            lane = slice(c * width, (c + 1) * width)
            mode = tail[t, :, lane].astype(jnp.float32)
            carry[c, here, :] = (sums[:, lanes:] * mode - sums[:, lane]).astype(jnp.bfloat16)

    @pl.when(gives_carry)
    def _():
        carry_copy.start()

    @pl.when(jnp.logical_not(takes_carry))
    def _():
        extra[...] = jnp.zeros_like(extra)

    def finish_own(i, _):
        sums = run[lasts[0, first_row + i]] + acc[block_rows(i), :]
        here = block_rows(first_row + i)
        for c in range(coords):
            lane = slice(c * width, (c + 1) * width)
            mode = wide[first_row + i, :, lane].astype(jnp.float32)
            base[c, here, :] = mode - 0.2 * (sums[:, lanes:] * mode - sums[:, lane])
        return 0

    lax.fori_loop(0, count, finish_own, 0)
    for turn in range(1, pair):
        far = lax.rem(half + turn, pair) * count

        def finish_other(i, _, far=far):
            sums = run[lasts[0, far + i]]
            here = block_rows(far + i)
            for c in range(coords):
                lane = slice(c * width, (c + 1) * width)
                mode = wide[far + i, :, lane].astype(jnp.float32)
                base[c, here, :] = -0.2 * (sums[:, lanes:] * mode - sums[:, lane])
            return 0

        lax.fori_loop(0, count, finish_other, 0)

    for c in range(coords):
        flipped[c] = modes_of(c).T

    tile = income.shape[2]
    per = share // tile

    def arrive(blocks_of):
        for j in blocks_of:
            for copy in gathers[j]:
                copy.wait()
        span = slice(starts[blocks_of[0]], starts[blocks_of[-1]] + sizes[blocks_of[-1]])
        turned[:, span] = low[span, :].astype(jnp.float32).T.astype(jnp.bfloat16)
        front = turned[:, span]
        gram = lax.dot_general(front, front, FAR, preferred_element_type=jnp.float32)
        gram = gram * -scale
        high = gram.astype(jnp.bfloat16)
        rest = (gram - high.astype(jnp.float32)).astype(jnp.bfloat16)
        grams = jnp.concatenate([high, rest], axis=1)

        def partial_update(c, start):
            here = ds(start, tile)
            across = flipped[c, :, here]
            hebb = dot(front, held[c, span, here])
            hebb = hebb + dot(grams, jnp.concatenate([across, across], axis=0))
            return rate * hebb.T + base[c, here, :]

        return partial_update

    early = parts // 2
    if early:
        partial_update = arrive(list(range(early)))
        for k in range(coords * verts // tile):
            c, start = k * tile // verts, k * tile % verts
            base[c, start : start + tile, :] = partial_update(c, start)
    partial_update = arrive(list(range(early, parts)))

    exchanges = []
    for turn in range(1, pair):
        other = lax.rem(half + turn, pair)
        for k in range(coords * per):
            c, start = k // per, other * share + (k % per) * tile
            outgo[turn - 1, k] = partial_update(c, start).astype(jnp.bfloat16)
            exchanges.append(
                pltpu.make_async_remote_copy(
                    src_ref=outgo.at[turn - 1, k],
                    dst_ref=income.at[turn - 1, k],
                    send_sem=send_u.at[turn - 1, k],
                    recv_sem=recv_u.at[turn - 1, k],
                    device_id={"batch": other},
                    device_id_type=MESH,
                )
            )
            exchanges[-1].start()
    for k in range(coords * per):
        c, start = k // per, half * share + (k % per) * tile
        base[c, ds(start, tile), :] = partial_update(c, start)

    @pl.when(gives_carry)
    def _():
        carry_copy.wait_send()

    @pl.when(takes_carry)
    def _():
        carry_copy.wait_recv()

    @pl.when(half == 0)
    def _():
        for c in range(coords):
            here = pl.ds(0, edge * side)
            base[c, here, :] = base[c, here, :] - 0.2 * extra[c].astype(jnp.float32)

    shares = []
    sums = jnp.zeros((8, width), jnp.float32)
    for k in range(coords * per):
        start = half * share + (k % per) * tile
        here = ds((k // per) * verts + start, tile)
        value = base[k // per, ds(start, tile), :]
        for turn in range(1, pair):
            exchanges[(turn - 1) * coords * per + k].wait()
            value = value + income[turn - 1, k].astype(jnp.float32)
        updated[here, :] = value.astype(jnp.bfloat16)
        sums = sums + jnp.sum((value * value).reshape(tile // 8, 8, width), axis=0)
        for turn in range(1, pair):
            shares.append(
                pltpu.make_async_remote_copy(
                    src_ref=updated.at[here],
                    dst_ref=updated.at[here],
                    send_sem=send_g.at[turn - 1, k],
                    recv_sem=recv_g.at[turn - 1, k],
                    device_id={"batch": lax.rem(half + turn, pair)},
                    device_id_type=MESH,
                )
            )
            shares[-1].start()
    mine = half * n + me
    slots[mine] = jnp.sum(sums, axis=0, keepdims=True)
    signals = []
    for turn in range(pair):
        for step in ([0] if turn else []) + far_first(n):
            at = turn * n + step
            signals.append(
                pltpu.make_async_remote_copy(
                    src_ref=slots.at[mine],
                    dst_ref=slots.at[mine],
                    send_sem=send_n.at[at],
                    recv_sem=recv_n.at[at],
                    device_id={
                        "patch": lax.rem(me + step, n),
                        "batch": lax.rem(half + turn, pair),
                    },
                    device_id_type=MESH,
                )
            )
            signals[-1].start()
    for copy in signals:
        copy.wait()
    squares = jnp.sum(slots[...], axis=0)
    norms[...] = jnp.sqrt(squares / coord_count + 1e-06)
    for copy in shares:
        copy.wait()


def step(planes, modes, blocks, columns, scale, rate, coord_count):
    n, pair = lax.axis_size("patch"), lax.axis_size("batch")
    coords, subjects, verts = planes.shape
    width = modes.shape[2]
    all_rows, per_row, side, _ = blocks.shape
    modes = modes.reshape(coords, all_rows, side, width)
    count = all_rows // pair
    parts = max(1, min(4, subjects // (8 * n)))
    sizes = [subjects // parts] * parts
    if parts == 4 and subjects % (64 * n) == 0:
        sizes = [subjects // 8 * units for units in (2, 2, 3, 1)]
    reach = GHOST * side
    lanes = (coords + 1) * width
    share = verts // pair
    tile = math.gcd(share, 1280)
    tiles = coords * share // tile
    dma = pltpu.SemaphoreType.DMA
    bf16, f32 = jnp.bfloat16, jnp.float32
    return pl.pallas_call(
        functools.partial(step_kernel, sizes, scale, rate, coord_count),
        out_shape=(
            jax.ShapeDtypeStruct((coords * verts, width), bf16),
            jax.ShapeDtypeStruct((1, width), f32),
            jax.ShapeDtypeStruct((subjects, width), bf16),
        ),
        in_specs=[HBM] * 4,
        out_specs=(VMEM,) * 3,
        scratch_shapes=[
            pltpu.VMEM((coords, subjects, verts), bf16),
            pltpu.VMEM((all_rows + GHOST, side, lanes), bf16),
            pltpu.VMEM((GHOST, side, coords * width), bf16),
            pltpu.VMEM((count, per_row, side, side), bf16),
            pltpu.SMEM(columns.shape, jnp.int32),
            pltpu.VMEM(columns.shape, jnp.int32),
            pltpu.VMEM(columns.shape, jnp.int32),
            pltpu.VMEM((2, all_rows), jnp.int32),
            pltpu.SMEM(columns.shape, jnp.int32),
            pltpu.SMEM((2, all_rows), jnp.int32),
            pltpu.VMEM((subjects, width), f32),
            pltpu.VMEM((subjects, width), WIRE),
            pltpu.VMEM((n, subjects // n, width), WIRE),
            pltpu.VMEM((1 + count * (per_row - 1), side, lanes), f32),
            pltpu.VMEM((count * side, lanes), f32),
            pltpu.VMEM((coords, verts, width), f32),
            pltpu.VMEM((width, subjects), bf16),
            pltpu.VMEM((coords, width, verts), bf16),
            pltpu.VMEM((pair - 1, tiles, tile, width), bf16),
            pltpu.VMEM((pair - 1, tiles, tile, width), bf16),
            pltpu.VMEM((coords, reach, width), bf16),
            pltpu.VMEM((coords, reach, width), bf16),
            pltpu.VMEM((n * pair, 1, width), f32),
            dma((coords,)),
            dma((coords, parts)),
            dma((5,)),
            dma((parts, n)),
            dma((parts, n)),
            dma((parts, n)),
            dma((parts, n)),
            dma((2,)),
            dma((2,)),
            dma((pair - 1, tiles)),
            dma((pair - 1, tiles)),
            dma((pair - 1, tiles)),
            dma((pair - 1, tiles)),
            dma((n * pair,)),
            dma((n * pair,)),
        ],
        compiler_params=pltpu.CompilerParams(
            collective_id=0, has_side_effects=True, vmem_limit_bytes=LIMIT
        ),
        name="step",
    )(*(pltpu.with_memory_space_constraint(x, pltpu.HBM) for x in (planes, modes, blocks, columns)))


def finish_kernel(updated, norm, low, out, norms, scores, held, wide, sems):
    inverse = 1.0 / norm[...]
    norms[...] = norm[...]
    pieces, rows, _ = held.shape
    wide[...] = low[...].astype(jnp.float32)
    copies = [pltpu.make_async_copy(wide, scores, sems.at[pieces])]
    copies[0].start()
    for k in range(pieces):
        value = updated[k * rows : (k + 1) * rows, :].astype(jnp.float32)
        held[k] = (value * inverse).astype(jnp.bfloat16)
        copies.append(pltpu.make_async_copy(held.at[k], out.at[pl.ds(k * rows, rows)], sems.at[k]))
        copies[-1].start()
    for copy in copies:
        copy.wait()


def finish(updated, norm, low):
    rows, width = updated.shape
    pieces = 6
    return pl.pallas_call(
        finish_kernel,
        out_shape=(
            jax.ShapeDtypeStruct(updated.shape, jnp.bfloat16),
            jax.ShapeDtypeStruct(norm.shape, jnp.float32),
            jax.ShapeDtypeStruct(low.shape, jnp.float32),
        ),
        in_specs=[VMEM] * 3,
        out_specs=(ANY, VMEM, ANY),
        scratch_shapes=[
            pltpu.VMEM((pieces, rows // pieces, width), jnp.bfloat16),
            pltpu.VMEM(low.shape, jnp.float32),
            pltpu.SemaphoreType.DMA((pieces + 1,)),
        ],
        compiler_params=pltpu.CompilerParams(vmem_limit_bytes=16 * 1024 * 1024),
        name="finish",
    )(updated, norm, low)


def body(subjects, basis_modes, laplace_blocks, columns):
    subject_count, coords, vert_count = subjects.shape
    mode_count = basis_modes.shape[2]
    n, pair = lax.axis_size("patch"), lax.axis_size("batch")
    coord_count = coords * vert_count * n
    scale = 1.0 / math.sqrt(coord_count)
    rate = 4.0 / (subject_count * pair)
    planes = subjects.transpose(1, 0, 2)
    updated, norm, low = step(
        planes, basis_modes, laplace_blocks, columns.T, scale, rate, coord_count
    )
    new_modes, norms, scores = finish(updated, norm, low)
    return (scores, new_modes.reshape(coords, vert_count, mode_count), norms.reshape(mode_count))


def solution(mesh):
    placed = (
        P(("groups", "batch"), None, "patch"),
        P(None, ("groups", "patch"), None),
        P("patch", None, None, None),
        P("patch", None),
    )
    return jax.shard_map(
        body,
        mesh=mesh,
        in_specs=placed,
        out_specs=(P(("groups", "batch"), None), P(None, ("groups", "patch"), None), P("groups")),
        check_vma=False,
    )
```
